32 devices in a mesh: drive: 2 (over y), tm: 4 (over z), mom: 2 (over x), col: 2 (over core).
Axes of the slice: x: 2, y: 2, z: 4, core: 2. Of those that a mesh axis runs over, the one named last changes fastest.
Arguments:
- propagators: float32 [8, 8, 384, 384], P(('drive', 'mom'), 'tm', None, 'col'), parts along dimension 0, as said below
- current_op: float32 [4, 384, 384], P('mom'), may hold values from -6 to 6
Outputs:
- spectrum: float32 [8, 2, 8, 384, 384], P(('drive', 'mom'), None, None, 'tm', 'col'), parts along dimension 0
The draws below stay inside these ranges and needn't reach their ends.
There are 2 independent parts, one for each index of `drive`. The reference program is written for one: setup_inputs(seed, part) draws one part's arguments, and reference() takes and returns one part's arrays. A program takes and returns all parts, laid end to end along the dimension named above; an argument that names none is the same for every part. Nothing has to cross between parts.
Inputs may be any that keep to these rules, and one draw needn't show every extreme that they name: Every matrix propagators[k, t] is orthogonal to float32 rounding, with dense entries.
All inputs are finite; a program needn't handle non-finite values.
Results may differ from the reference program's by a relative error of at most 0.0003.
Values sent between devices are 32-bit elements; how exact they have to be, the bound alone decides.
No kernel may reach another device: no remote copies, remote signals or barrier semaphores. Data moves between devices by JAX's collectives and lax.ppermute only.
A program may use at most 64 MiB of HBM per device.

```python
import math
import jax
import jax.numpy as jnp
from jax import lax

K = 4
M = 384
TIME = 8


def draw_propagators(key, part):
    base = jax.random.normal(jax.random.fold_in(key, 7), (K, TIME, M, M), jnp.float32)
    ortho, upper = jnp.linalg.qr(base)
    diag = jnp.diagonal(upper, axis1=2, axis2=3)
    signs = jnp.where(diag >= 0, 1.0, -1.0).astype(jnp.float32)
    return (ortho * signs[:, :, None, :]).astype(jnp.float32)


def block_scale(stream_key, dims, shards, smallest, largest):
    def one(position, parts):
        draws = jax.random.uniform(jax.random.fold_in(jax.random.fold_in(stream_key, 6), position), (parts,), jnp.float32, smallest / len(shards), largest / len(shards))
        return jnp.repeat(jnp.exp(draws), dims[position] // parts).reshape((-1,) + (1,) * (len(dims) - position - 1))

    factor_of = one(*shards[0])
    for cut in shards[1:]:
        factor_of = factor_of * one(*cut)
    return factor_of


def centred(key, dims, scale, bound, shards=(), kind=jnp.bfloat16):
    array = jax.random.normal(key, dims, jnp.float32) * scale
    if len(shards) > 0:
        array = block_scale(key, dims, shards, -0.22, 0.18) * array
    return jnp.clip(array, min=-bound, max=bound).astype(kind)


def setup_inputs(seed: int = 0, part: int = 0) -> dict:
    key_of = jax.random.split(jax.random.key(seed), 3)
    part_splits = jax.random.split(jax.random.fold_in(key_of[2], part), 3)
    return {
        "propagators": draw_propagators(jax.random.fold_in(jax.random.fold_in(key_of[2], part), 71), part),
        "current_op": centred(key_of[1], (K, M, M), 1.0, 6.0, ((0, 2),), jnp.float32),
    }


def one_momentum(args):
    units, operator = args
    sym = 0.5 * (operator + operator.T)

    def advance(prefix, unit):
        prefix = jnp.dot(unit, prefix, precision=lax.Precision.HIGHEST)
        weighted = jnp.dot(sym, prefix, precision=lax.Precision.HIGHEST)
        heis = jnp.dot(prefix.T, weighted, precision=lax.Precision.HIGHEST)
        return (prefix, heis)
    start = jnp.eye(M, dtype=jnp.float32)
    _, history = lax.scan(advance, start, units)
    transformed = jnp.fft.fft(history, axis=0) / math.sqrt(TIME)
    return jnp.stack([jnp.real(transformed), jnp.imag(transformed)]).astype(jnp.float32)

def reference(propagators, current_op):
    return lax.map(one_momentum, (propagators, current_op))
```

```python
import math

import jax
import jax.numpy as jnp
from jax import lax
from jax.experimental import pallas as pl
from jax.experimental.pallas import tpu as pltpu
from jax.sharding import PartitionSpec as P

CHUNKS = 3


def prefix_2(value, axis, join, neutral):
    count, mine = (lax.axis_size(axis), lax.axis_index(axis))
    pieces = lax.all_gather(value, axis)
    running = jnp.full_like(value, 0) + jnp.asarray(neutral, value.dtype)

    def turn(position, running):
        longer = join(running, pieces[position])
        return jnp.where(position < mine, longer, running)

    return lax.fori_loop(0, count - 1, turn, running)


def multiply(left, right):
    return jnp.einsum("kab,kbc->kac", left, right, precision=lax.Precision.HIGHEST)


def later_first(earlier, later):
    return multiply(later, earlier)


def chain_step(carry, unit):
    nxt = multiply(unit, carry)
    return (nxt, nxt)


def spectrum_block(block):
    length = block.shape[1]
    freq = lax.broadcasted_iota(jnp.int32, (length, length), 0)
    times = lax.broadcasted_iota(jnp.int32, (length, length), 1)
    phase = 2.0 * math.pi / length * (freq * times % length).astype(jnp.float32)
    scale = 1.0 / math.sqrt(length)
    cosine = jnp.cos(phase) * scale
    sine = -jnp.sin(phase) * scale
    real = jnp.einsum("ft,ktrc->kfrc", cosine, block, precision=lax.Precision.HIGHEST)
    imag = jnp.einsum("ft,ktrc->kfrc", sine, block, precision=lax.Precision.HIGHEST)
    return jnp.stack([real, imag], axis=1)


def general_body(propagators, current_op):
    sym = 0.5 * (current_op + jnp.swapaxes(current_op, 1, 2))
    whole = lax.all_to_all(propagators, "col", split_axis=1, concat_axis=3, tiled=True)
    kdev = whole.shape[0]
    order = whole.shape[2]
    units = jnp.moveaxis(whole, 1, 0)
    total = units[0]
    identity = jnp.broadcast_to(jnp.eye(order, dtype=jnp.float32), total.shape)
    carry_in = prefix_2(total, ("tm", "col"), later_first, identity)
    _, applied = lax.scan(chain_step, carry_in, units)
    prefix = jnp.moveaxis(applied, 0, 1)
    weighted = jnp.einsum("kab,ksbc->ksac", sym, prefix, precision=lax.Precision.HIGHEST)
    n_rows = lax.axis_size("tm")
    n_cols = lax.axis_size("col")
    row_width = order // n_rows
    col_width = order // n_cols
    slices = prefix.shape[1]
    left = prefix.reshape(kdev, slices, order, n_rows, row_width)
    right = weighted.reshape(kdev, slices, order, n_cols, col_width)
    heis = jnp.einsum("ksbir,ksbjq->ksijrq", left, right, precision=lax.Precision.HIGHEST)
    heis = heis.reshape(kdev, slices, n_rows * n_cols, row_width, col_width)
    block = lax.all_to_all(heis, ("tm", "col"), split_axis=2, concat_axis=1, tiled=True)
    return spectrum_block(block[:, :, 0])


def halves(x):
    high = x.astype(jnp.bfloat16)
    return high, (x - high.astype(jnp.float32)).astype(jnp.bfloat16)


def as_left(x):
    high, low = halves(x)
    return jnp.concatenate([high, high, low], axis=1)


def as_right(x):
    high, low = halves(x)
    return jnp.concatenate([high, low, high], axis=0)


def as_right_t(x):
    high, low = halves(x)
    return jnp.concatenate([high, low, high], axis=1)


def product(left, right):
    return jnp.dot(left, right, preferred_element_type=jnp.float32)


def product_t(left, right):
    dims = (((1,), (1,)), ((), ()))
    return lax.dot_general(left, right, dims, preferred_element_type=jnp.float32)


VMEM = pl.BlockSpec(memory_space=pltpu.VMEM)


def local_call(kernel, outs, args, scratch=(), name=None):
    return pl.pallas_call(
        kernel,
        out_shape=[jax.ShapeDtypeStruct(s, jnp.float32) for s in outs],
        in_specs=[VMEM] * len(args),
        out_specs=[VMEM] * len(outs),
        scratch_shapes=list(scratch),
        name=name,
    )(*args)


def start_kernel(mine_ref, got_ref, op_ref, a0_ref, a1_ref, sym_ref, *prod_refs):
    core = lax.axis_index("col")
    part = got_ref.shape[1]
    for s, a_ref in enumerate((a0_ref, a1_ref)):
        a_ref[pl.ds(pl.multiple_of(core * part, 8), part), :] = mine_ref[core, s]
        a_ref[pl.ds(pl.multiple_of((1 - core) * part, 8), part), :] = got_ref[s]
    right = as_right(a1_ref[...])
    row = 0
    for p_ref in prod_refs:
        rows = p_ref.shape[0]
        p_ref[...] = product(as_left(a0_ref[row:row + rows, :]), right)
        row += rows
    op = op_ref[core]
    sym_ref[...] = 0.5 * (op + op.T)


def hop_kernel(place, in_ref, *refs):
    *prod_refs, out_ref = refs

    @pl.when(lax.axis_index("tm") == place)
    def _():
        b = jnp.concatenate([r[...] for r in prod_refs], axis=0)
        out_ref[...] = product(as_left(in_ref[...]), as_right(b))


def heis_kernel(place, count, chunks, *refs):
    ins, outs, (r_ref, s_ref) = refs[:2 + 2 * chunks], refs[2 + 2 * chunks:-2], refs[-2:]
    a0_ref, sym_ref = ins[:2]
    before, after = ins[2:2 + chunks], ins[2 + chunks:]

    @pl.when(lax.axis_index("tm") == place)
    def _():
        order = a0_ref.shape[0]
        rows = order // count
        step = order // chunks
        for q in range(chunks):
            r_ref[0, q * step:(q + 1) * step, :] = before[q][...]
            r_ref[2, q * step:(q + 1) * step, :] = after[q][...]
        s_ref[...] = as_right(sym_ref[...])
        if place == 0:
            r_ref[1] = a0_ref[...]
        else:
            r_ref[1] = product(as_left(r_ref[0]), as_right(a0_ref[...]))
        for i in ((1, 2) if place == 0 else (0, 1, 2)):
            top = 0 if i >= 1 else place * rows
            bottom = order if i <= 1 else (place + 1) * rows
            weighted = product(as_left(r_ref[i, top:bottom, :]), s_ref[...])
            heis = product_t(as_left(weighted), as_right_t(r_ref[i]))
            for to in range(top // rows, bottom // rows):
                first = (1 if place == 0 else 0) if to >= place else 1
                outs[to][i - first] = heis[to * rows - top:(to + 1) * rows - top, :]


def sent_slices(place, to):
    first = max(2 * place - 1, 0) if to >= place else 2 * place
    last = 2 * place if to > place else 2 * place + 1
    return list(range(first, last + 1))


def gather_kernel(count, *refs):
    ins, (keep_ref, send_ref) = refs[:-2], refs[-2:]
    core = lax.axis_index("col")
    width = keep_ref.shape[2]
    for to in range(count):
        @pl.when(lax.axis_index("tm") == to)
        def _(to=to):
            for c in range(2):
                @pl.when(core == c)
                def _(c=c):
                    for place in range(count):
                        for i, t in enumerate(sent_slices(place, to)):
                            block = ins[place * count + to][i]
                            keep_ref[t] = block[:, c * width:(c + 1) * width]
                            send_ref[t] = block[:, (1 - c) * width:(2 - c) * width]


def spectrum_kernel(keep_ref, got_ref, out_ref):
    core = lax.axis_index("col")
    length, rows, width = keep_ref.shape
    scale = 1.0 / math.sqrt(length)
    step = 8

    def cosine(n):
        return scale * math.cos(2.0 * math.pi * (n % length) / length)

    def sine(n):
        return scale * math.sin(2.0 * math.pi * (n % length) / length)

    def block(source, k, row):
        here = pl.ds(pl.multiple_of(row * step, step), step)
        values = [source[t, here, :] for t in range(length)]
        for f in range(length // 2 + 1):
            real = sum(cosine(f * t) * values[t] for t in range(length))
            out_ref[k, 0, f, here, :] = real
            mirrored = (length - f) % length
            if mirrored != f:
                imag = sum(-sine(f * t) * values[t] for t in range(1, length))
                out_ref[k, 0, mirrored, here, :] = real
                out_ref[k, 1, f, here, :] = imag
                out_ref[k, 1, mirrored, here, :] = -imag
            else:
                imag = sum(-sine(f * t) * values[t] for t in range(length))
                out_ref[k, 1, f, here, :] = imag

    def turn(row, carry):
        block(keep_ref, core, row)
        block(got_ref, 1 - core, row)
        return carry

    lax.fori_loop(0, rows // step, turn, 0)


def paired_body(propagators, current_op):
    count = lax.axis_size("tm")
    core = lax.axis_index("col")
    flipped = jnp.swapaxes(propagators, 2, 3)
    kdev, slices, part, order = flipped.shape
    rows = order // count
    swap = [(0, 1), (1, 0)]
    other = lax.dynamic_index_in_dim(flipped, 1 - core, 0, keepdims=False)
    got = lax.ppermute(other, "col", swap)
    step = order // CHUNKS
    square, chunk = (order, order), (step, order)
    a0, a1, sym, *prod = local_call(
        start_kernel, [square] * 3 + [chunk] * CHUNKS, (flipped, got, current_op), name="start"
    )
    moved = [[None] * count for _ in range(count)]

    def send(place, to):
        moved[place][to] = lax.ppermute(outs[place][to], "tm", [(place, to)])

    outs = []
    before, after = prod, prod
    for place in range(count):
        if place > 0:
            before = [lax.ppermute(x, "tm", [(place - 1, place)]) for x in after]
            after = [
                local_call(lambda *r, p=place: hop_kernel(p, *r), [chunk], (x, *prod), name="hop")[0]
                for x in before
            ]
        shapes = [(len(sent_slices(place, to)), rows, order) for to in range(count)]
        outs.append(
            local_call(
                lambda *r, p=place: heis_kernel(p, count, CHUNKS, *r),
                shapes,
                (a0, sym, *before, *after),
                scratch=[pltpu.VMEM((3, order, order), jnp.float32), pltpu.VMEM((3 * order, order), jnp.bfloat16)],
                name="heis",
            )
        )
        moved[place][place] = outs[place][place]
        for to in range(count):
            if to != place:
                send(place, to)
    pieces = [moved[place][to] for place in range(count) for to in range(count)]
    width = order // 2
    keep, give = local_call(
        lambda *r: gather_kernel(count, *r), [(count * slices, rows, width)] * 2, pieces, name="gather"
    )
    taken = lax.ppermute(give, "col", swap)
    return local_call(
        spectrum_kernel, [(kdev, 2, count * slices, rows, width)], (keep, taken), name="spectrum"
    )[0]


def solution(mesh):
    def body(propagators, current_op):
        kdev, slices, order, _ = propagators.shape
        count = mesh.shape["tm"]
        paired = kdev == 2 and mesh.shape["col"] == 2 and slices == 2 and count > 1
        if paired and order % (16 * CHUNKS) == 0 and order % (16 * count) == 0:
            return paired_body(propagators, current_op)
        return general_body(propagators, current_op)

    return jax.shard_map(
        body,
        mesh=mesh,
        in_specs=(P(("drive", "mom"), "tm", None, "col"), P("mom", None, None)),
        out_specs=P(("drive", "mom"), None, None, "tm", "col"),
        check_vma=False,
    )
```

```python
import math

import jax
import jax.numpy as jnp
from jax import lax
from jax.experimental import pallas as pl
from jax.experimental.pallas import tpu as pltpu
from jax.sharding import PartitionSpec as P

CHUNKS = 3
GRANT = pltpu.CompilerParams(vmem_limit_bytes=20 * 2**20)


def prefix_2(value, axis, join, neutral):
    count, mine = (lax.axis_size(axis), lax.axis_index(axis))
    pieces = lax.all_gather(value, axis)
    running = jnp.full_like(value, 0) + jnp.asarray(neutral, value.dtype)

    def turn(position, running):
        longer = join(running, pieces[position])
        return jnp.where(position < mine, longer, running)

    return lax.fori_loop(0, count - 1, turn, running)


def multiply(left, right):
    return jnp.einsum("kab,kbc->kac", left, right, precision=lax.Precision.HIGHEST)


def later_first(earlier, later):
    return multiply(later, earlier)


def chain_step(carry, unit):
    nxt = multiply(unit, carry)
    return (nxt, nxt)


def spectrum_block(block):
    length = block.shape[1]
    freq = lax.broadcasted_iota(jnp.int32, (length, length), 0)
    times = lax.broadcasted_iota(jnp.int32, (length, length), 1)
    phase = 2.0 * math.pi / length * (freq * times % length).astype(jnp.float32)
    scale = 1.0 / math.sqrt(length)
    cosine = jnp.cos(phase) * scale
    sine = -jnp.sin(phase) * scale
    real = jnp.einsum("ft,ktrc->kfrc", cosine, block, precision=lax.Precision.HIGHEST)
    imag = jnp.einsum("ft,ktrc->kfrc", sine, block, precision=lax.Precision.HIGHEST)
    return jnp.stack([real, imag], axis=1)


def general_body(propagators, current_op):
    sym = 0.5 * (current_op + jnp.swapaxes(current_op, 1, 2))
    whole = lax.all_to_all(propagators, "col", split_axis=1, concat_axis=3, tiled=True)
    kdev = whole.shape[0]
    order = whole.shape[2]
    units = jnp.moveaxis(whole, 1, 0)
    total = units[0]
    identity = jnp.broadcast_to(jnp.eye(order, dtype=jnp.float32), total.shape)
    carry_in = prefix_2(total, ("tm", "col"), later_first, identity)
    _, applied = lax.scan(chain_step, carry_in, units)
    prefix = jnp.moveaxis(applied, 0, 1)
    weighted = jnp.einsum("kab,ksbc->ksac", sym, prefix, precision=lax.Precision.HIGHEST)
    n_rows = lax.axis_size("tm")
    n_cols = lax.axis_size("col")
    row_width = order // n_rows
    col_width = order // n_cols
    slices = prefix.shape[1]
    left = prefix.reshape(kdev, slices, order, n_rows, row_width)
    right = weighted.reshape(kdev, slices, order, n_cols, col_width)
    heis = jnp.einsum("ksbir,ksbjq->ksijrq", left, right, precision=lax.Precision.HIGHEST)
    heis = heis.reshape(kdev, slices, n_rows * n_cols, row_width, col_width)
    block = lax.all_to_all(heis, ("tm", "col"), split_axis=2, concat_axis=1, tiled=True)
    return spectrum_block(block[:, :, 0])


def halves(x):
    high = x.astype(jnp.bfloat16)
    return high, (x - high.astype(jnp.float32)).astype(jnp.bfloat16)


def as_left(x):
    high, low = halves(x)
    return jnp.concatenate([high, high, low], axis=1)


def as_right(x):
    high, low = halves(x)
    return jnp.concatenate([high, low, high], axis=0)


def as_right_t(x):
    high, low = halves(x)
    return jnp.concatenate([high, low, high], axis=1)


def product(left, right):
    return jnp.dot(left, right, preferred_element_type=jnp.float32)


def product_t(left, right):
    dims = (((1,), (1,)), ((), ()))
    return lax.dot_general(left, right, dims, preferred_element_type=jnp.float32)


VMEM = pl.BlockSpec(memory_space=pltpu.VMEM)


def local_call(kernel, outs, args, scratch=(), name=None, outside=()):
    near = [
        x if i in outside else pltpu.with_memory_space_constraint(x, pltpu.VMEM)
        for i, x in enumerate(args)
    ]
    return pl.pallas_call(
        kernel,
        out_shape=[pltpu.VMEM(s, jnp.float32) for s in outs],
        in_specs=[VMEM] * len(args),
        out_specs=[VMEM] * len(outs),
        scratch_shapes=list(scratch),
        compiler_params=GRANT,
        name=name,
    )(*near)


def start_kernel(mine_ref, got_ref, op_ref, a0_ref, a1_ref, sym_ref, *prod_refs):
    core = lax.axis_index("col")
    part = got_ref.shape[1]
    for s, a_ref in enumerate((a0_ref, a1_ref)):
        a_ref[pl.ds(pl.multiple_of(core * part, 8), part), :] = mine_ref[core, s]
        a_ref[pl.ds(pl.multiple_of((1 - core) * part, 8), part), :] = got_ref[s]
    right = as_right(a1_ref[...])
    row = 0
    for p_ref in prod_refs:
        rows = p_ref.shape[0]
        p_ref[...] = product(as_left(a0_ref[row:row + rows, :]), right)
        row += rows
    op = op_ref[core]
    sym_ref[...] = 0.5 * (op + op.T)


def hop_kernel(place, in_ref, *refs):
    *prod_refs, out_ref = refs

    @pl.when(lax.axis_index("tm") == place)
    def _():
        b = jnp.concatenate([r[...] for r in prod_refs], axis=0)
        out_ref[...] = product(as_left(in_ref[...]), as_right(b))


def heis_kernel(place, count, chunks, *refs):
    ins, outs, (r_ref, s_ref) = refs[:2 + 2 * chunks], refs[2 + 2 * chunks:-2], refs[-2:]
    a0_ref, sym_ref = ins[:2]
    before, after = ins[2:2 + chunks], ins[2 + chunks:]

    @pl.when(lax.axis_index("tm") == place)
    def _():
        order = a0_ref.shape[0]
        rows = order // count
        step = order // chunks
        for q in range(chunks):
            r_ref[0, q * step:(q + 1) * step, :] = before[q][...]
            r_ref[2, q * step:(q + 1) * step, :] = after[q][...]
        s_ref[...] = as_right(sym_ref[...])
        if place == 0:
            r_ref[1] = a0_ref[...]
        else:
            r_ref[1] = product(as_left(r_ref[0]), as_right(a0_ref[...]))
        for i in ((1, 2) if place == 0 else (0, 1, 2)):
            top = 0 if i >= 1 else place * rows
            bottom = order if i <= 1 else (place + 1) * rows
            weighted = product(as_left(r_ref[i, top:bottom, :]), s_ref[...])
            heis = product_t(as_left(weighted), as_right_t(r_ref[i]))
            for to in range(top // rows, bottom // rows):
                first = (1 if place == 0 else 0) if to >= place else 1
                outs[to][i - first] = heis[to * rows - top:(to + 1) * rows - top, :]


def sent_slices(place, to):
    first = max(2 * place - 1, 0) if to >= place else 2 * place
    last = 2 * place if to > place else 2 * place + 1
    return list(range(first, last + 1))


def gather_kernel(count, *refs):
    ins, (keep_ref, send_ref) = refs[:-2], refs[-2:]
    core = lax.axis_index("col")
    width = keep_ref.shape[2]
    for to in range(count):
        @pl.when(lax.axis_index("tm") == to)
        def _(to=to):
            for c in range(2):
                @pl.when(core == c)
                def _(c=c):
                    for place in range(count):
                        for i, t in enumerate(sent_slices(place, to)):
                            block = ins[place * count + to][i]
                            keep_ref[t] = block[:, c * width:(c + 1) * width]
                            send_ref[t] = block[:, (1 - c) * width:(2 - c) * width]


def spectrum_kernel(keep_ref, got_ref, out_ref):
    core = lax.axis_index("col")
    length, rows, width = keep_ref.shape
    scale = 1.0 / math.sqrt(length)
    step = 8

    def cosine(n):
        return scale * math.cos(2.0 * math.pi * (n % length) / length)

    def sine(n):
        return scale * math.sin(2.0 * math.pi * (n % length) / length)

    def block(source, k, row):
        here = pl.ds(pl.multiple_of(row * step, step), step)
        values = [source[t, here, :] for t in range(length)]
        for f in range(length // 2 + 1):
            real = sum(cosine(f * t) * values[t] for t in range(length))
            out_ref[k, 0, f, here, :] = real
            mirrored = (length - f) % length
            if mirrored != f:
                imag = sum(-sine(f * t) * values[t] for t in range(1, length))
                out_ref[k, 0, mirrored, here, :] = real
                out_ref[k, 1, f, here, :] = imag
                out_ref[k, 1, mirrored, here, :] = -imag
            else:
                imag = sum(-sine(f * t) * values[t] for t in range(length))
                out_ref[k, 1, f, here, :] = imag

    def turn(row, carry):
        block(keep_ref, core, row)
        block(got_ref, 1 - core, row)
        return carry

    lax.fori_loop(0, rows // step, turn, 0)


def paired_body(propagators, current_op):
    count = lax.axis_size("tm")
    core = lax.axis_index("col")
    flipped = jnp.swapaxes(propagators, 2, 3)
    kdev, slices, part, order = flipped.shape
    rows = order // count
    swap = [(0, 1), (1, 0)]
    other = lax.dynamic_index_in_dim(flipped, 1 - core, 0, keepdims=False)
    got = lax.ppermute(other, "col", swap)
    step = order // CHUNKS
    square, chunk = (order, order), (step, order)
    a0, a1, sym, *prod = local_call(
        start_kernel, [square] * 3 + [chunk] * CHUNKS, (flipped, got, current_op), name="start", outside=(0, 2)
    )
    moved = [[None] * count for _ in range(count)]

    def send(place, to):
        moved[place][to] = lax.ppermute(outs[place][to], "tm", [(place, to)])

    outs = []
    before, after = prod, prod
    for place in range(count):
        if place > 0:
            before = [lax.ppermute(x, "tm", [(place - 1, place)]) for x in after]
            after = [
                local_call(lambda *r, p=place: hop_kernel(p, *r), [chunk], (x, *prod), name="hop")[0]
                for x in before
            ]
        shapes = [(len(sent_slices(place, to)), rows, order) for to in range(count)]
        outs.append(
            local_call(
                lambda *r, p=place: heis_kernel(p, count, CHUNKS, *r),
                shapes,
                (a0, sym, *before, *after),
                scratch=[pltpu.VMEM((3, order, order), jnp.float32), pltpu.VMEM((3 * order, order), jnp.bfloat16)],
                name="heis",
            )
        )
        moved[place][place] = outs[place][place]
        for to in range(count):
            if to != place:
                send(place, to)
    pieces = [moved[place][to] for place in range(count) for to in range(count)]
    width = order // 2
    keep, give = local_call(
        lambda *r: gather_kernel(count, *r), [(count * slices, rows, width)] * 2, pieces, name="gather"
    )
    taken = lax.ppermute(give, "col", swap)
    return pl.pallas_call(
        spectrum_kernel,
        out_shape=jax.ShapeDtypeStruct((kdev, 2, count * slices, rows, width), jnp.float32),
        in_specs=[VMEM] * 2,
        out_specs=VMEM,
        compiler_params=GRANT,
        name="spectrum",
    )(*(pltpu.with_memory_space_constraint(x, pltpu.VMEM) for x in (keep, taken)))


def solution(mesh):
    def body(propagators, current_op):
        kdev, slices, order, _ = propagators.shape
        count = mesh.shape["tm"]
        paired = kdev == 2 and mesh.shape["col"] == 2 and slices == 2 and count > 1
        if paired and order % (16 * CHUNKS) == 0 and order % (16 * count) == 0:
            return paired_body(propagators, current_op)
        return general_body(propagators, current_op)

    return jax.shard_map(
        body,
        mesh=mesh,
        in_specs=(P(("drive", "mom"), "tm", None, "col"), P("mom", None, None)),
        out_specs=P(("drive", "mom"), None, None, "tm", "col"),
        check_vma=False,
    )
```

```python
import math

import jax
import jax.numpy as jnp
from jax import lax
from jax.experimental import pallas as pl
from jax.experimental.pallas import tpu as pltpu
from jax.sharding import PartitionSpec as P

CHUNKS = 3
GRANT = pltpu.CompilerParams(vmem_limit_bytes=20 * 2**20)


def prefix_2(value, axis, join, neutral):
    count, mine = (lax.axis_size(axis), lax.axis_index(axis))
    pieces = lax.all_gather(value, axis)
    running = jnp.full_like(value, 0) + jnp.asarray(neutral, value.dtype)

    def turn(position, running):
        longer = join(running, pieces[position])
        return jnp.where(position < mine, longer, running)

    return lax.fori_loop(0, count - 1, turn, running)


def multiply(left, right):
    return jnp.einsum("kab,kbc->kac", left, right, precision=lax.Precision.HIGHEST)


def later_first(earlier, later):
    return multiply(later, earlier)


def chain_step(carry, unit):
    nxt = multiply(unit, carry)
    return (nxt, nxt)


def spectrum_block(block):
    length = block.shape[1]
    freq = lax.broadcasted_iota(jnp.int32, (length, length), 0)
    times = lax.broadcasted_iota(jnp.int32, (length, length), 1)
    phase = 2.0 * math.pi / length * (freq * times % length).astype(jnp.float32)
    scale = 1.0 / math.sqrt(length)
    cosine = jnp.cos(phase) * scale
    sine = -jnp.sin(phase) * scale
    real = jnp.einsum("ft,ktrc->kfrc", cosine, block, precision=lax.Precision.HIGHEST)
    imag = jnp.einsum("ft,ktrc->kfrc", sine, block, precision=lax.Precision.HIGHEST)
    return jnp.stack([real, imag], axis=1)


def general_body(propagators, current_op):
    sym = 0.5 * (current_op + jnp.swapaxes(current_op, 1, 2))
    whole = lax.all_to_all(propagators, "col", split_axis=1, concat_axis=3, tiled=True)
    kdev = whole.shape[0]
    order = whole.shape[2]
    units = jnp.moveaxis(whole, 1, 0)
    total = units[0]
    identity = jnp.broadcast_to(jnp.eye(order, dtype=jnp.float32), total.shape)
    carry_in = prefix_2(total, ("tm", "col"), later_first, identity)
    _, applied = lax.scan(chain_step, carry_in, units)
    prefix = jnp.moveaxis(applied, 0, 1)
    weighted = jnp.einsum("kab,ksbc->ksac", sym, prefix, precision=lax.Precision.HIGHEST)
    n_rows = lax.axis_size("tm")
    n_cols = lax.axis_size("col")
    row_width = order // n_rows
    col_width = order // n_cols
    slices = prefix.shape[1]
    left = prefix.reshape(kdev, slices, order, n_rows, row_width)
    right = weighted.reshape(kdev, slices, order, n_cols, col_width)
    heis = jnp.einsum("ksbir,ksbjq->ksijrq", left, right, precision=lax.Precision.HIGHEST)
    heis = heis.reshape(kdev, slices, n_rows * n_cols, row_width, col_width)
    block = lax.all_to_all(heis, ("tm", "col"), split_axis=2, concat_axis=1, tiled=True)
    return spectrum_block(block[:, :, 0])


def halves(x):
    high = x.astype(jnp.bfloat16)
    return high, (x - high.astype(jnp.float32)).astype(jnp.bfloat16)


def as_left(x):
    high, low = halves(x)
    return jnp.concatenate([high, high, low], axis=1)


def as_right(x):
    high, low = halves(x)
    return jnp.concatenate([high, low, high], axis=0)


def as_right_t(x):
    high, low = halves(x)
    return jnp.concatenate([high, low, high], axis=1)


def product(left, right):
    return jnp.dot(left, right, preferred_element_type=jnp.float32)


def product_t(left, right):
    dims = (((1,), (1,)), ((), ()))
    return lax.dot_general(left, right, dims, preferred_element_type=jnp.float32)


VMEM = pl.BlockSpec(memory_space=pltpu.VMEM)


def local_call(kernel, outs, args, scratch=(), name=None, outside=()):
    near = [
        x if i in outside else pltpu.with_memory_space_constraint(x, pltpu.VMEM)
        for i, x in enumerate(args)
    ]
    return pl.pallas_call(
        kernel,
        out_shape=[pltpu.VMEM(s, jnp.float32) for s in outs],
        in_specs=[VMEM] * len(args),
        out_specs=[VMEM] * len(outs),
        scratch_shapes=list(scratch),
        compiler_params=GRANT,
        name=name,
    )(*near)


def pick_kernel(in_ref, mine_ref, other_ref, sems):
    core = lax.axis_index("col")
    copies = [
        pltpu.make_async_copy(in_ref.at[1 - core], other_ref, sems.at[0]),
        pltpu.make_async_copy(in_ref.at[core], mine_ref, sems.at[1]),
    ]
    for copy in copies:
        copy.start()
    for copy in copies:
        copy.wait()


def start_kernel(mine_ref, got_ref, a0_ref, *refs):
    *prod_refs, a1_ref = refs
    core = lax.axis_index("col")
    part = got_ref.shape[1]
    for s, a_ref in enumerate((a0_ref, a1_ref)):
        a_ref[pl.ds(pl.multiple_of(core * part, 8), part), :] = mine_ref[s]
        a_ref[pl.ds(pl.multiple_of((1 - core) * part, 8), part), :] = got_ref[s]
    right = as_right(a1_ref[...])
    row = 0
    for p_ref in prod_refs:
        rows = p_ref.shape[0]
        p_ref[...] = product(as_left(a0_ref[row:row + rows, :]), right)
        row += rows


def packed(x):
    third = x.shape[0] // 3
    lower = jnp.concatenate([x[third:2 * third, third:], x[2 * third:, 2 * third:]], axis=1)
    return jnp.concatenate([x[:third, :], lower], axis=0)


def unpacked(x):
    third = x.shape[0] // 2
    top = x[:third, :]
    b11, b12, b22 = (x[third:, i * third:(i + 1) * third] for i in range(3))
    middle = jnp.concatenate([top[:, third:2 * third].T, b11, b12], axis=1)
    bottom = jnp.concatenate([top[:, 2 * third:].T, b12.T, b22], axis=1)
    return jnp.concatenate([top, middle, bottom], axis=0)


def local_kernel(count, chunks, *refs):
    a0_ref, *prod_refs, op_ref = refs[:chunks + 2]
    sym_ref, g0_ref, g1_ref, pack_ref, own_ref, *row_refs = refs[chunks + 2:]
    place = lax.axis_index("tm")
    op = op_ref[lax.axis_index("col")]
    sym = 0.5 * (op + op.T)
    sym_ref[...] = sym
    right = as_right(sym)
    a0 = a0_ref[...]
    b = jnp.concatenate([r[...] for r in prod_refs], axis=0)
    for x, g_ref in ((a0, g0_ref), (b, g1_ref)):
        g_ref[...] = product_t(as_left(product(as_left(x), right)), as_right_t(x))
    rows = own_ref.shape[1]

    @pl.when(place >= 2)
    def _():
        pack_ref[0] = packed(g0_ref[...])
        pack_ref[1] = packed(g1_ref[...])

    @pl.when(place == 0)
    def _():
        own_ref[0] = g0_ref[:rows, :]
        own_ref[1] = g1_ref[:rows, :]
        for i, row_ref in enumerate(row_refs):
            row_ref[0] = g0_ref[(i + 1) * rows:(i + 2) * rows, :]


def hop_kernel(place, in_ref, *refs):
    *prod_refs, out_ref = refs

    @pl.when(lax.axis_index("tm") == place)
    def _():
        b = jnp.concatenate([r[...] for r in prod_refs], axis=0)
        out_ref[...] = product(as_left(in_ref[...]), as_right(b))


def joined(out_ref, parts):
    row = 0
    for part in parts:
        out_ref[row:row + part.shape[0], :] = part[...]
        row += part.shape[0]


def rows_out(outs, wanted, heis, top, rows):
    for to, position in wanted.items():
        outs[to][position] = heis[to * rows - top:(to + 1) * rows - top, :]


def heis_kernel(place, count, chunks, *refs):
    sym_ref, g0_ref, g1_ref = refs[:3]
    before = refs[3:3 + chunks]
    outs, r_ref, t_ref = refs[3 + chunks:-2], refs[-2], refs[-1]
    outs = dict(zip(heis_receivers(place, count), outs))

    @pl.when(lax.axis_index("tm") == place)
    def _():
        order = sym_ref.shape[0]
        rows = order // count
        joined(r_ref, before)
        t_ref[...] = as_right_t(r_ref[...])
        for i, middle_ref in enumerate((sym_ref, g0_ref, g1_ref)):
            t = 2 * place - 1 + i
            wanted = {to: heis_slices(place, to).index(t) for to in outs if t in heis_slices(place, to)}
            top, bottom = min(wanted) * rows, (max(wanted) + 1) * rows
            weighted = product(as_left(r_ref[top:bottom, :]), as_right(middle_ref[...]))
            rows_out(outs, wanted, product_t(as_left(weighted), t_ref[...]), top, rows)


def ahead_kernel(place, count, chunks, *refs):
    pack_ref, *after = refs[:1 + chunks]
    outs, r_ref, t_ref = refs[1 + chunks:-2], refs[-2], refs[-1]

    @pl.when(lax.axis_index("tm") == place)
    def _():
        order = pack_ref.shape[2]
        rows = order // count
        joined(r_ref, after)
        t_ref[...] = as_right_t(r_ref[...])
        left = as_left(r_ref[:(place + 1) * rows, :])
        for i in range(2):
            weighted = product(left, as_right(unpacked(pack_ref[i])))
            heis = product_t(as_left(weighted), t_ref[...])
            rows_out(outs, {to: i for to in range(place + 1)}, heis, 0, rows)


def heis_slices(place, to):
    if to > place:
        return [2 * place - 1, 2 * place]
    if to == place:
        return [2 * place - 1, 2 * place, 2 * place + 1]
    return [2 * place, 2 * place + 1]


def heis_receivers(place, count):
    return [0] * (place == 1) + list(range(place, count))


def gather_kernel(plan, *refs):
    ins, (keep_ref, send_ref) = refs[:-2], refs[-2:]
    core = lax.axis_index("col")
    width = keep_ref.shape[2]
    for to, entries in enumerate(plan):
        @pl.when(lax.axis_index("tm") == to)
        def _(entries=entries):
            for c in range(2):
                @pl.when(core == c)
                def _(c=c):
                    for source, slices in entries:
                        for i, t in enumerate(slices):
                            block = ins[source][i]
                            keep_ref[t] = block[:, c * width:(c + 1) * width]
                            send_ref[t] = block[:, (1 - c) * width:(2 - c) * width]


def spectrum_kernel(keep_ref, got_ref, out_ref):
    core = lax.axis_index("col")
    length, rows, width = keep_ref.shape
    scale = 1.0 / math.sqrt(length)
    step = 8

    def cosine(n):
        return scale * math.cos(2.0 * math.pi * (n % length) / length)

    def sine(n):
        return scale * math.sin(2.0 * math.pi * (n % length) / length)

    def block(source, k, row):
        here = pl.ds(pl.multiple_of(row * step, step), step)
        values = [source[t, here, :] for t in range(length)]
        for f in range(length // 2 + 1):
            real = sum(cosine(f * t) * values[t] for t in range(length))
            out_ref[k, 0, f, here, :] = real
            mirrored = (length - f) % length
            if mirrored != f:
                imag = sum(-sine(f * t) * values[t] for t in range(1, length))
                out_ref[k, 0, mirrored, here, :] = real
                out_ref[k, 1, f, here, :] = imag
                out_ref[k, 1, mirrored, here, :] = -imag
            else:
                imag = sum(-sine(f * t) * values[t] for t in range(length))
                out_ref[k, 1, f, here, :] = imag

    def turn(row, carry):
        block(keep_ref, core, row)
        block(got_ref, 1 - core, row)
        return carry

    lax.fori_loop(0, rows // step, turn, 0)


def paired_body(propagators, current_op):
    count = lax.axis_size("tm")
    flipped = jnp.swapaxes(propagators, 2, 3)
    kdev, slices, part, order = flipped.shape
    rows = order // count
    step = order // CHUNKS
    square, chunk = (order, order), (step, order)
    swap = [(0, 1), (1, 0)]
    scratch = [pltpu.VMEM(square, jnp.float32), pltpu.VMEM((order, 3 * order), jnp.bfloat16)]

    mine, other = pl.pallas_call(
        pick_kernel,
        out_shape=[pltpu.VMEM((slices, part, order), jnp.float32)] * 2,
        in_specs=[pl.BlockSpec(memory_space=pl.ANY)],
        out_specs=[VMEM] * 2,
        scratch_shapes=[pltpu.SemaphoreType.DMA((2,))],
        compiler_params=GRANT,
        name="pick",
    )(flipped)
    got = lax.ppermute(other, "col", swap)
    a0, *prod = local_call(
        start_kernel, [square] + [chunk] * CHUNKS, (mine, got),
        scratch=[pltpu.VMEM(square, jnp.float32)], name="start",
    )

    def along(x, hop, name):
        with jax.named_scope(name):
            return lax.ppermute(x, "tm", [hop] if isinstance(hop, tuple) else hop)

    arrays, plan = [], [[] for _ in range(count)]

    def keep(x, to, ts):
        plan[to].append((len(arrays), ts))
        arrays.append(x)

    before = [along(x, (0, 1), f"hop1_{i}") for i, x in enumerate(prod)]
    shapes = [square] * 3 + [(2, 2 * (order // 3), order), (2, rows, order)] + [(1, rows, order)] * (count - 1)
    with jax.named_scope("local"):
        sym, g0, g1, pack, own, *firsts = local_call(
            lambda *r: local_kernel(count, CHUNKS, *r), shapes, (a0, *prod, current_op),
            name="local", outside=(CHUNKS + 1,),
        )
    ahead = along(pack, [(j, j - 1) for j in range(2, count)], "pack")
    keep(own, 0, [0, 1])
    for to in range(1, count):
        keep(along(firsts[to - 1], (0, to), f"first_{to}"), to, [0])
    for place in range(1, count):
        with jax.named_scope(f"hop_{place}"):
            after = [
                local_call(lambda *r, p=place: hop_kernel(p, *r), [chunk], (x, *prod), name="hop")[0]
                for x in before
            ]
        if place + 1 < count:
            following = [along(x, (place, place + 1), f"hop{place + 1}_{i}") for i, x in enumerate(after)]
        receivers = heis_receivers(place, count)
        with jax.named_scope(f"heis_{place}"):
            outs = local_call(
                lambda *r, p=place: heis_kernel(p, count, CHUNKS, *r),
                [(len(heis_slices(place, to)), rows, order) for to in receivers],
                (sym, g0, g1, *before), scratch=scratch, name="heis",
            )
        for to, x in zip(receivers, outs):
            keep(x if to == place else along(x, (place, to), f"known_{place}_{to}"), to, heis_slices(place, to))
        if place + 1 < count:
            with jax.named_scope(f"ahead_{place}"):
                outs = local_call(
                    lambda *r, p=place: ahead_kernel(p, count, CHUNKS, *r),
                    [(2, rows, order)] * (place + 1), (ahead, *after), scratch=scratch, name="ahead",
                )
            for to, x in enumerate(outs):
                ts = [2 * place + 2, 2 * place + 3]
                keep(x if to == place else along(x, (place, to), f"ahead_{place}_{to}"), to, ts)
            before = following
    width = order // 2
    kept, give = local_call(
        lambda *r: gather_kernel(plan, *r), [(count * slices, rows, width)] * 2, arrays, name="gather"
    )
    taken = lax.ppermute(give, "col", swap)
    return pl.pallas_call(
        spectrum_kernel,
        out_shape=jax.ShapeDtypeStruct((kdev, 2, count * slices, rows, width), jnp.float32),
        in_specs=[VMEM] * 2,
        out_specs=VMEM,
        compiler_params=GRANT,
        name="spectrum",
    )(*(pltpu.with_memory_space_constraint(x, pltpu.VMEM) for x in (kept, taken)))


def solution(mesh):
    def body(propagators, current_op):
        kdev, slices, order, _ = propagators.shape
        count = mesh.shape["tm"]
        paired = kdev == 2 and mesh.shape["col"] == 2 and slices == 2 and count > 2
        if paired and order % 384 == 0 and order % (16 * CHUNKS) == 0 and order % (16 * count) == 0:
            return paired_body(propagators, current_op)
        return general_body(propagators, current_op)

    return jax.shard_map(
        body,
        mesh=mesh,
        in_specs=(P(("drive", "mom"), "tm", None, "col"), P("mom", None, None)),
        out_specs=P(("drive", "mom"), None, None, "tm", "col"),
        check_vma=False,
    )
```

```python
import math

import jax
import jax.numpy as jnp
from jax import lax
from jax.experimental import pallas as pl
from jax.experimental.pallas import tpu as pltpu
from jax.sharding import PartitionSpec as P


CHUNKS = 3
GRANT = pltpu.CompilerParams(vmem_limit_bytes=20 * 2**20)


def prefix_2(value, axis, join, neutral):
    count, mine = (lax.axis_size(axis), lax.axis_index(axis))
    pieces = lax.all_gather(value, axis)
    running = jnp.full_like(value, 0) + jnp.asarray(neutral, value.dtype)

    def turn(position, running):
        longer = join(running, pieces[position])
        return jnp.where(position < mine, longer, running)

    return lax.fori_loop(0, count - 1, turn, running)


def multiply(left, right):
    return jnp.einsum("kab,kbc->kac", left, right, precision=lax.Precision.HIGHEST)


def later_first(earlier, later):
    return multiply(later, earlier)


def chain_step(carry, unit):
    nxt = multiply(unit, carry)
    return (nxt, nxt)


def spectrum_block(block):
    length = block.shape[1]
    freq = lax.broadcasted_iota(jnp.int32, (length, length), 0)
    times = lax.broadcasted_iota(jnp.int32, (length, length), 1)
    phase = 2.0 * math.pi / length * (freq * times % length).astype(jnp.float32)
    scale = 1.0 / math.sqrt(length)
    cosine = jnp.cos(phase) * scale
    sine = -jnp.sin(phase) * scale
    real = jnp.einsum("ft,ktrc->kfrc", cosine, block, precision=lax.Precision.HIGHEST)
    imag = jnp.einsum("ft,ktrc->kfrc", sine, block, precision=lax.Precision.HIGHEST)
    return jnp.stack([real, imag], axis=1)


def general_body(propagators, current_op):
    sym = 0.5 * (current_op + jnp.swapaxes(current_op, 1, 2))
    whole = lax.all_to_all(propagators, "col", split_axis=1, concat_axis=3, tiled=True)
    kdev = whole.shape[0]
    order = whole.shape[2]
    units = jnp.moveaxis(whole, 1, 0)
    total = units[0]
    identity = jnp.broadcast_to(jnp.eye(order, dtype=jnp.float32), total.shape)
    carry_in = prefix_2(total, ("tm", "col"), later_first, identity)
    _, applied = lax.scan(chain_step, carry_in, units)
    prefix = jnp.moveaxis(applied, 0, 1)
    weighted = jnp.einsum("kab,ksbc->ksac", sym, prefix, precision=lax.Precision.HIGHEST)
    n_rows = lax.axis_size("tm")
    n_cols = lax.axis_size("col")
    row_width = order // n_rows
    col_width = order // n_cols
    slices = prefix.shape[1]
    left = prefix.reshape(kdev, slices, order, n_rows, row_width)
    right = weighted.reshape(kdev, slices, order, n_cols, col_width)
    heis = jnp.einsum("ksbir,ksbjq->ksijrq", left, right, precision=lax.Precision.HIGHEST)
    heis = heis.reshape(kdev, slices, n_rows * n_cols, row_width, col_width)
    block = lax.all_to_all(heis, ("tm", "col"), split_axis=2, concat_axis=1, tiled=True)
    return spectrum_block(block[:, :, 0])


def halves(x):
    high = x.astype(jnp.bfloat16)
    return high, (x - high.astype(jnp.float32)).astype(jnp.bfloat16)


def as_left(x):
    high, low = halves(x)
    return jnp.concatenate([high, high, low], axis=1)


def as_right(x):
    high, low = halves(x)
    return jnp.concatenate([high, low, high], axis=0)


def as_right_t(x):
    high, low = halves(x)
    return jnp.concatenate([high, low, high], axis=1)


def product(left, right):
    return jnp.dot(left, right, preferred_element_type=jnp.float32)


def product_t(left, right):
    dims = (((1,), (1,)), ((), ()))
    return lax.dot_general(left, right, dims, preferred_element_type=jnp.float32)


VMEM = pl.BlockSpec(memory_space=pltpu.VMEM)


def local_call(kernel, outs, args, scratch=(), outside=()):
    near = [
        x if i in outside else pltpu.with_memory_space_constraint(x, pltpu.VMEM)
        for i, x in enumerate(args)
    ]
    return pl.pallas_call(
        kernel,
        out_shape=[pltpu.VMEM(s, jnp.float32) for s in outs],
        in_specs=[VMEM] * len(args),
        out_specs=[VMEM] * len(outs),
        scratch_shapes=list(scratch),
        compiler_params=GRANT,
    )(*near)


def pick_kernel(in_ref, mine_ref, other_ref, sems):
    core = lax.axis_index("col")
    copies = [
        pltpu.make_async_copy(in_ref.at[1 - core], other_ref, sems.at[0]),
        pltpu.make_async_copy(in_ref.at[core], mine_ref, sems.at[1]),
    ]
    for copy in copies:
        copy.start()
    for copy in copies:
        copy.wait()


def start_kernel(mine_ref, got_ref, a0_ref, *refs):
    *prod_refs, a1_ref = refs
    core = lax.axis_index("col")
    part = got_ref.shape[1]
    for s, a_ref in enumerate((a0_ref, a1_ref)):
        a_ref[pl.ds(pl.multiple_of(core * part, 8), part), :] = mine_ref[s]
        a_ref[pl.ds(pl.multiple_of((1 - core) * part, 8), part), :] = got_ref[s]
    right = as_right(a1_ref[...])
    row = 0
    for p_ref in prod_refs:
        rows = p_ref.shape[0]
        p_ref[...] = product(as_left(a0_ref[row:row + rows, :]), right)
        row += rows


def packed(x):
    third = x.shape[0] // 3
    lower = jnp.concatenate([x[third:2 * third, third:], x[2 * third:, 2 * third:]], axis=1)
    return jnp.concatenate([x[:third, :], lower], axis=0)


def unpacked(x):
    third = x.shape[0] // 2
    top = x[:third, :]
    b11, b12, b22 = (x[third:, i * third:(i + 1) * third] for i in range(3))
    middle = jnp.concatenate([top[:, third:2 * third].T, b11, b12], axis=1)
    bottom = jnp.concatenate([top[:, 2 * third:].T, b12.T, b22], axis=1)
    return jnp.concatenate([top, middle, bottom], axis=0)


def local_kernel(chunks, *refs):
    a0_ref, *prod_refs, op_ref = refs[:chunks + 2]
    sym_ref, g0_ref, g1_ref, pack_ref, own_ref, *row_refs = refs[chunks + 2:]
    place = lax.axis_index("tm")
    op = op_ref[lax.axis_index("col")]
    sym = 0.5 * (op + op.T)
    sym_ref[...] = sym
    right = as_right(sym)
    a0 = a0_ref[...]
    b = jnp.concatenate([r[...] for r in prod_refs], axis=0)
    for x, g_ref in ((a0, g0_ref), (b, g1_ref)):
        g_ref[...] = product_t(as_left(product(as_left(x), right)), as_right_t(x))
    rows = own_ref.shape[1]

    @pl.when(place >= 2)
    def _():
        pack_ref[0] = packed(g0_ref[...])
        pack_ref[1] = packed(g1_ref[...])

    @pl.when(place == 0)
    def _():
        own_ref[0] = g0_ref[:rows, :]
        own_ref[1] = g1_ref[:rows, :]
        for i, row_ref in enumerate(row_refs):
            row_ref[0] = g0_ref[(i + 1) * rows:(i + 2) * rows, :]


def hop_kernel(place, in_ref, *refs):
    *prod_refs, out_ref = refs

    @pl.when(lax.axis_index("tm") == place)
    def _():
        b = jnp.concatenate([r[...] for r in prod_refs], axis=0)
        out_ref[...] = product(as_left(in_ref[...]), as_right(b))


def joined(out_ref, parts):
    row = 0
    for part in parts:
        out_ref[row:row + part.shape[0], :] = part[...]
        row += part.shape[0]


def rows_out(outs, wanted, heis, top, rows):
    for to, position in wanted.items():
        outs[to][position] = heis[to * rows - top:(to + 1) * rows - top, :]


def heis_kernel(place, count, chunks, *refs):
    sym_ref, g0_ref, g1_ref = refs[:3]
    before = refs[3:3 + chunks]
    outs, r_ref, t_ref = refs[3 + chunks:-2], refs[-2], refs[-1]
    outs = dict(zip(heis_receivers(place, count), outs))

    @pl.when(lax.axis_index("tm") == place)
    def _():
        order = sym_ref.shape[0]
        rows = order // count
        joined(r_ref, before)
        t_ref[...] = as_right_t(r_ref[...])
        for i, middle_ref in enumerate((sym_ref, g0_ref, g1_ref)):
            t = 2 * place - 1 + i
            wanted = {to: heis_slices(place, to).index(t) for to in outs if t in heis_slices(place, to)}
            top, bottom = min(wanted) * rows, (max(wanted) + 1) * rows
            weighted = product(as_left(r_ref[top:bottom, :]), as_right(middle_ref[...]))
            rows_out(outs, wanted, product_t(as_left(weighted), t_ref[...]), top, rows)


def ahead_kernel(place, count, chunks, *refs):
    pack_ref, *after = refs[:1 + chunks]
    outs, r_ref, t_ref = refs[1 + chunks:-2], refs[-2], refs[-1]

    @pl.when(lax.axis_index("tm") == place)
    def _():
        order = pack_ref.shape[2]
        rows = order // count
        joined(r_ref, after)
        t_ref[...] = as_right_t(r_ref[...])
        left = as_left(r_ref[:(place + 1) * rows, :])
        for i in range(2):
            weighted = product(left, as_right(unpacked(pack_ref[i])))
            heis = product_t(as_left(weighted), t_ref[...])
            rows_out(outs, {to: i for to in range(place + 1)}, heis, 0, rows)


def heis_slices(place, to):
    if to > place:
        return [2 * place - 1, 2 * place]
    if to == place:
        return [2 * place - 1, 2 * place, 2 * place + 1]
    return [2 * place, 2 * place + 1]


def heis_receivers(place, count):
    return [0] * (place == 1) + list(range(place, count))


def gather_kernel(plan, *refs):
    ins, (keep_ref, send_ref) = refs[:-2], refs[-2:]
    core = lax.axis_index("col")
    width = keep_ref.shape[2]
    for to, entries in enumerate(plan):
        @pl.when(lax.axis_index("tm") == to)
        def _(entries=entries):
            for c in range(2):
                @pl.when(core == c)
                def _(c=c):
                    for source, slices in entries:
                        for i, t in enumerate(slices):
                            block = ins[source][i]
                            keep_ref[t] = block[:, c * width:(c + 1) * width]
                            send_ref[t] = block[:, (1 - c) * width:(2 - c) * width]


def spectrum_kernel(keep_ref, got_ref, out_ref):
    core = lax.axis_index("col")
    length, rows, _ = keep_ref.shape
    scale = 1.0 / math.sqrt(length)
    step = 8

    def cosine(n):
        return scale * math.cos(2.0 * math.pi * (n % length) / length)

    def sine(n):
        return scale * math.sin(2.0 * math.pi * (n % length) / length)

    def block(source, k, row):
        here = pl.ds(pl.multiple_of(row * step, step), step)
        values = [source[t, here, :] for t in range(length)]
        for f in range(length // 2 + 1):
            real = sum(cosine(f * t) * values[t] for t in range(length))
            out_ref[k, 0, f, here, :] = real
            mirrored = (length - f) % length
            if mirrored != f:
                imag = sum(-sine(f * t) * values[t] for t in range(1, length))
                out_ref[k, 0, mirrored, here, :] = real
                out_ref[k, 1, f, here, :] = imag
                out_ref[k, 1, mirrored, here, :] = -imag
            else:
                imag = sum(-sine(f * t) * values[t] for t in range(length))
                out_ref[k, 1, f, here, :] = imag

    def turn(row, carry):
        block(keep_ref, core, row)
        block(got_ref, 1 - core, row)
        return carry

    lax.fori_loop(0, rows // step, turn, 0)


def paired_body(propagators, current_op):
    count = lax.axis_size("tm")
    flipped = jnp.swapaxes(propagators, 2, 3)
    kdev, slices, part, order = flipped.shape
    rows = order // count
    step = order // CHUNKS
    square, chunk = (order, order), (step, order)
    swap = [(0, 1), (1, 0)]
    scratch = [pltpu.VMEM(square, jnp.float32), pltpu.VMEM((order, 3 * order), jnp.bfloat16)]

    mine, other = pl.pallas_call(
        pick_kernel,
        out_shape=[pltpu.VMEM((slices, part, order), jnp.float32)] * 2,
        in_specs=[pl.BlockSpec(memory_space=pltpu.HBM)],
        out_specs=[VMEM] * 2,
        scratch_shapes=[pltpu.SemaphoreType.DMA((2,))],
        compiler_params=GRANT,
        name="pick",
    )(pltpu.with_memory_space_constraint(flipped, pltpu.HBM))
    got = lax.ppermute(other, "col", swap)
    a0, *prod = local_call(
        start_kernel, [square] + [chunk] * CHUNKS, (mine, got),
        scratch=[pltpu.VMEM(square, jnp.float32)],
    )

    def along(x, hop):
        return lax.ppermute(x, "tm", [hop] if isinstance(hop, tuple) else hop)

    arrays, plan = [], [[] for _ in range(count)]

    def keep(x, to, ts):
        plan[to].append((len(arrays), ts))
        arrays.append(x)

    before = [along(x, (0, 1)) for x in prod]
    shapes = [square] * 3 + [(2, 2 * (order // 3), order), (2, rows, order)] + [(1, rows, order)] * (count - 1)
    sym, g0, g1, pack, own, *firsts = local_call(
        lambda *r: local_kernel(CHUNKS, *r), shapes, (a0, *prod, current_op),
        outside=(CHUNKS + 1,),
    )
    ahead = along(pack, [(j, j - 1) for j in range(2, count)])
    keep(own, 0, [0, 1])
    for to in range(1, count):
        keep(along(firsts[to - 1], (0, to)), to, [0])
    for place in range(1, count):
        after = []
        for x in before if place + 1 < count else ():
            after += local_call(lambda *r, p=place: hop_kernel(p, *r), [chunk], (x, *prod))
        if place + 1 < count:
            following = [along(x, (place, place + 1)) for x in after]
        receivers = heis_receivers(place, count)
        outs = local_call(
            lambda *r, p=place: heis_kernel(p, count, CHUNKS, *r),
            [(len(heis_slices(place, to)), rows, order) for to in receivers],
            (sym, g0, g1, *before), scratch=scratch,
        )
        for to, x in zip(receivers, outs):
            keep(x if to == place else along(x, (place, to)), to, heis_slices(place, to))
        if place + 1 < count:
            outs = local_call(
                lambda *r, p=place: ahead_kernel(p, count, CHUNKS, *r),
                [(2, rows, order)] * (place + 1), (ahead, *after), scratch=scratch,
            )
            for to, x in enumerate(outs):
                ts = [2 * place + 2, 2 * place + 3]
                keep(x if to == place else along(x, (place, to)), to, ts)
            before = following
    width = order // 2
    kept, give = local_call(lambda *r: gather_kernel(plan, *r), [(count * slices, rows, width)] * 2, arrays)
    taken = lax.ppermute(give, "col", swap)
    return pl.pallas_call(
        spectrum_kernel,
        out_shape=jax.ShapeDtypeStruct((kdev, 2, count * slices, rows, width), jnp.float32),
        in_specs=[VMEM] * 2,
        out_specs=VMEM,
        compiler_params=GRANT,
        name="spectrum",
    )(*(pltpu.with_memory_space_constraint(x, pltpu.VMEM) for x in (kept, taken)))


def is_paired(mesh, kdev, slices, order):
    count = mesh.shape["tm"]
    fits = kdev == 2 and mesh.shape["col"] == 2 and slices == 2 and count > 2
    return fits and order % 384 == 0 and order % (16 * CHUNKS) == 0 and order % (16 * count) == 0


def solution(mesh):
    def body(propagators, current_op):
        kdev, slices, order, _ = propagators.shape
        if is_paired(mesh, kdev, slices, order):
            return paired_body(propagators, current_op)
        return general_body(propagators, current_op)

    return jax.shard_map(
        body,
        mesh=mesh,
        in_specs=(P(("drive", "mom"), "tm", None, "col"), P("mom", None, None)),
        out_specs=P(("drive", "mom"), None, None, "tm", "col"),
        check_vma=False,
    )
```

```python
import math

import jax
import jax.numpy as jnp
from jax import lax
from jax.experimental import pallas as pl
from jax.experimental.pallas import tpu as pltpu
from jax.sharding import PartitionSpec as P


CHUNKS = 3
GRANT = pltpu.CompilerParams(vmem_limit_bytes=20 * 2**20)


def prefix_2(value, axis, join, neutral):
    count, mine = (lax.axis_size(axis), lax.axis_index(axis))
    pieces = lax.all_gather(value, axis)
    running = jnp.full_like(value, 0) + jnp.asarray(neutral, value.dtype)

    def turn(position, running):
        longer = join(running, pieces[position])
        return jnp.where(position < mine, longer, running)

    return lax.fori_loop(0, count - 1, turn, running)


def multiply(left, right):
    return jnp.einsum("kab,kbc->kac", left, right, precision=lax.Precision.HIGHEST)


def later_first(earlier, later):
    return multiply(later, earlier)


def chain_step(carry, unit):
    nxt = multiply(unit, carry)
    return (nxt, nxt)


def spectrum_block(block):
    length = block.shape[1]
    freq = lax.broadcasted_iota(jnp.int32, (length, length), 0)
    times = lax.broadcasted_iota(jnp.int32, (length, length), 1)
    phase = 2.0 * math.pi / length * (freq * times % length).astype(jnp.float32)
    scale = 1.0 / math.sqrt(length)
    cosine = jnp.cos(phase) * scale
    sine = -jnp.sin(phase) * scale
    real = jnp.einsum("ft,ktrc->kfrc", cosine, block, precision=lax.Precision.HIGHEST)
    imag = jnp.einsum("ft,ktrc->kfrc", sine, block, precision=lax.Precision.HIGHEST)
    return jnp.stack([real, imag], axis=1)


def general_body(propagators, current_op):
    sym = 0.5 * (current_op + jnp.swapaxes(current_op, 1, 2))
    whole = lax.all_to_all(propagators, "col", split_axis=1, concat_axis=3, tiled=True)
    kdev = whole.shape[0]
    order = whole.shape[2]
    units = jnp.moveaxis(whole, 1, 0)
    total = units[0]
    identity = jnp.broadcast_to(jnp.eye(order, dtype=jnp.float32), total.shape)
    carry_in = prefix_2(total, ("tm", "col"), later_first, identity)
    _, applied = lax.scan(chain_step, carry_in, units)
    prefix = jnp.moveaxis(applied, 0, 1)
    weighted = jnp.einsum("kab,ksbc->ksac", sym, prefix, precision=lax.Precision.HIGHEST)
    n_rows = lax.axis_size("tm")
    n_cols = lax.axis_size("col")
    row_width = order // n_rows
    col_width = order // n_cols
    slices = prefix.shape[1]
    left = prefix.reshape(kdev, slices, order, n_rows, row_width)
    right = weighted.reshape(kdev, slices, order, n_cols, col_width)
    heis = jnp.einsum("ksbir,ksbjq->ksijrq", left, right, precision=lax.Precision.HIGHEST)
    heis = heis.reshape(kdev, slices, n_rows * n_cols, row_width, col_width)
    block = lax.all_to_all(heis, ("tm", "col"), split_axis=2, concat_axis=1, tiled=True)
    return spectrum_block(block[:, :, 0])


def halves(x):
    high = x.astype(jnp.bfloat16)
    return high, (x - high.astype(jnp.float32)).astype(jnp.bfloat16)


def as_left(x):
    high, low = halves(x)
    return jnp.concatenate([high, high, low], axis=1)


def as_right(x):
    high, low = halves(x)
    return jnp.concatenate([high, low, high], axis=0)


def as_right_t(x):
    high, low = halves(x)
    return jnp.concatenate([high, low, high], axis=1)


def product(left, right):
    return jnp.dot(left, right, preferred_element_type=jnp.float32)


def product_t(left, right):
    dims = (((1,), (1,)), ((), ()))
    return lax.dot_general(left, right, dims, preferred_element_type=jnp.float32)


VMEM = pl.BlockSpec(memory_space=pltpu.VMEM)


def local_call(kernel, outs, args, scratch=(), outside=()):
    near = [
        x if i in outside else pltpu.with_memory_space_constraint(x, pltpu.VMEM)
        for i, x in enumerate(args)
    ]
    return pl.pallas_call(
        kernel,
        out_shape=[pltpu.VMEM(s, jnp.float32) for s in outs],
        in_specs=[VMEM] * len(args),
        out_specs=[VMEM] * len(outs),
        scratch_shapes=list(scratch),
        compiler_params=GRANT,
    )(*near)


def pick_kernel(own, in_ref, out_ref, sem):
    core = lax.axis_index("col")
    copy = pltpu.make_async_copy(in_ref.at[core if own else 1 - core], out_ref, sem)
    copy.start()
    copy.wait()


def start_kernel(mine_ref, got_ref, a0_ref, *refs):
    *prod_refs, a1_ref = refs
    core = lax.axis_index("col")
    part = got_ref.shape[1]
    for s, a_ref in enumerate((a0_ref, a1_ref)):
        a_ref[pl.ds(pl.multiple_of(core * part, 8), part), :] = mine_ref[s]
        a_ref[pl.ds(pl.multiple_of((1 - core) * part, 8), part), :] = got_ref[s]
    right = as_right(a1_ref[...])
    row = 0
    for p_ref in prod_refs:
        rows = p_ref.shape[0]
        p_ref[...] = product(as_left(a0_ref[row:row + rows, :]), right)
        row += rows


def packed(x):
    third = x.shape[0] // 3
    lower = jnp.concatenate([x[third:2 * third, third:], x[2 * third:, 2 * third:]], axis=1)
    return jnp.concatenate([x[:third, :], lower], axis=0)


def unpacked(x):
    third = x.shape[0] // 2
    top = x[:third, :]
    b11, b12, b22 = (x[third:, i * third:(i + 1) * third] for i in range(3))
    middle = jnp.concatenate([top[:, third:2 * third].T, b11, b12], axis=1)
    bottom = jnp.concatenate([top[:, 2 * third:].T, b12.T, b22], axis=1)
    return jnp.concatenate([top, middle, bottom], axis=0)


def local_kernel(chunks, *refs):
    a0_ref, *prod_refs, op_ref = refs[:chunks + 2]
    sym_ref, g0_ref, g1_ref, pack_ref, own_ref, *row_refs = refs[chunks + 2:]
    place = lax.axis_index("tm")
    op = op_ref[lax.axis_index("col")]
    sym = 0.5 * (op + op.T)
    sym_ref[...] = sym
    right = as_right(sym)
    a0 = a0_ref[...]
    b = jnp.concatenate([r[...] for r in prod_refs], axis=0)
    for x, g_ref in ((a0, g0_ref), (b, g1_ref)):
        g_ref[...] = product_t(as_left(product(as_left(x), right)), as_right_t(x))
    rows = own_ref.shape[1]

    @pl.when(place >= 2)
    def _():
        pack_ref[0] = packed(g0_ref[...])
        pack_ref[1] = packed(g1_ref[...])

    @pl.when(place == 0)
    def _():
        own_ref[0] = g0_ref[:rows, :]
        own_ref[1] = g1_ref[:rows, :]
        for i, row_ref in enumerate(row_refs):
            row_ref[0] = g0_ref[(i + 1) * rows:(i + 2) * rows, :]


def hop_kernel(place, in_ref, *refs):
    *prod_refs, out_ref = refs

    @pl.when(lax.axis_index("tm") == place)
    def _():
        b = jnp.concatenate([r[...] for r in prod_refs], axis=0)
        out_ref[...] = product(as_left(in_ref[...]), as_right(b))


def joined(out_ref, parts):
    row = 0
    for part in parts:
        out_ref[row:row + part.shape[0], :] = part[...]
        row += part.shape[0]


def rows_out(outs, wanted, heis, top, rows):
    for to, position in wanted.items():
        outs[to][position] = heis[to * rows - top:(to + 1) * rows - top, :]


def heis_kernel(place, count, chunks, *refs):
    sym_ref, g0_ref, g1_ref = refs[:3]
    before = refs[3:3 + chunks]
    outs, r_ref, t_ref = refs[3 + chunks:-2], refs[-2], refs[-1]
    outs = dict(zip(heis_receivers(place, count), outs))

    @pl.when(lax.axis_index("tm") == place)
    def _():
        order = sym_ref.shape[0]
        rows = order // count
        joined(r_ref, before)
        t_ref[...] = as_right_t(r_ref[...])
        for i, middle_ref in enumerate((sym_ref, g0_ref, g1_ref)):
            t = 2 * place - 1 + i
            wanted = {to: heis_slices(place, to).index(t) for to in outs if t in heis_slices(place, to)}
            top, bottom = min(wanted) * rows, (max(wanted) + 1) * rows
            weighted = product(as_left(r_ref[top:bottom, :]), as_right(middle_ref[...]))
            rows_out(outs, wanted, product_t(as_left(weighted), t_ref[...]), top, rows)


def ahead_kernel(place, count, chunks, *refs):
    pack_ref, *after = refs[:1 + chunks]
    outs, r_ref, t_ref = refs[1 + chunks:-2], refs[-2], refs[-1]

    @pl.when(lax.axis_index("tm") == place)
    def _():
        order = pack_ref.shape[2]
        rows = order // count
        joined(r_ref, after)
        t_ref[...] = as_right_t(r_ref[...])
        left = as_left(r_ref[:(place + 1) * rows, :])
        for i in range(2):
            weighted = product(left, as_right(unpacked(pack_ref[i])))
            heis = product_t(as_left(weighted), t_ref[...])
            rows_out(outs, {to: i for to in range(place + 1)}, heis, 0, rows)


def heis_slices(place, to):
    if to > place:
        return [2 * place - 1, 2 * place]
    if to == place:
        return [2 * place - 1, 2 * place, 2 * place + 1]
    return [2 * place, 2 * place + 1]


def heis_receivers(place, count):
    return [0] * (place == 1) + list(range(place, count))


def gather_kernel(plan, *refs):
    ins, (keep_ref, send_ref) = refs[:-2], refs[-2:]
    core = lax.axis_index("col")
    width = keep_ref.shape[2]
    for to, entries in enumerate(plan):
        @pl.when(lax.axis_index("tm") == to)
        def _(entries=entries):
            for c in range(2):
                @pl.when(core == c)
                def _(c=c):
                    for source, slices in entries:
                        for i, t in enumerate(slices):
                            block = ins[source][i]
                            keep_ref[t] = block[:, c * width:(c + 1) * width]
                            send_ref[t] = block[:, (1 - c) * width:(2 - c) * width]


def spectrum_kernel(keep_ref, got_ref, out_ref):
    core = lax.axis_index("col")
    length, rows, _ = keep_ref.shape
    scale = 1.0 / math.sqrt(length)
    step = 8

    def cosine(n):
        return scale * math.cos(2.0 * math.pi * (n % length) / length)

    def sine(n):
        return scale * math.sin(2.0 * math.pi * (n % length) / length)

    def block(source, k, row):
        here = pl.ds(pl.multiple_of(row * step, step), step)
        values = [source[t, here, :] for t in range(length)]
        for f in range(length // 2 + 1):
            real = sum(cosine(f * t) * values[t] for t in range(length))
            out_ref[k, 0, f, here, :] = real
            mirrored = (length - f) % length
            if mirrored != f:
                imag = sum(-sine(f * t) * values[t] for t in range(1, length))
                out_ref[k, 0, mirrored, here, :] = real
                out_ref[k, 1, f, here, :] = imag
                out_ref[k, 1, mirrored, here, :] = -imag
            else:
                imag = sum(-sine(f * t) * values[t] for t in range(length))
                out_ref[k, 1, f, here, :] = imag

    def turn(row, carry):
        block(keep_ref, core, row)
        block(got_ref, 1 - core, row)
        return carry

    lax.fori_loop(0, rows // step, turn, 0)


def paired_body(propagators, current_op):
    count = lax.axis_size("tm")
    flipped = jnp.swapaxes(propagators, 2, 3)
    kdev, slices, part, order = flipped.shape
    rows = order // count
    step = order // CHUNKS
    square, chunk = (order, order), (step, order)
    swap = [(0, 1), (1, 0)]
    scratch = [pltpu.VMEM(square, jnp.float32), pltpu.VMEM((order, 3 * order), jnp.bfloat16)]

    def pick(own):
        return pl.pallas_call(
            lambda *r: pick_kernel(own, *r),
            out_shape=pltpu.VMEM((slices, part, order), jnp.float32),
            in_specs=[pl.BlockSpec(memory_space=pltpu.HBM)],
            out_specs=VMEM,
            scratch_shapes=[pltpu.SemaphoreType.DMA],
            compiler_params=GRANT,
        )(pltpu.with_memory_space_constraint(flipped, pltpu.HBM))

    got = lax.ppermute(pick(False), "col", swap)
    mine = pick(True)
    a0, *prod = local_call(
        start_kernel, [square] + [chunk] * CHUNKS, (mine, got),
        scratch=[pltpu.VMEM(square, jnp.float32)],
    )

    def along(x, hop):
        return lax.ppermute(x, "tm", [hop] if isinstance(hop, tuple) else hop)

    arrays, plan = [], [[] for _ in range(count)]

    def keep(x, to, ts):
        plan[to].append((len(arrays), ts))
        arrays.append(x)

    before = [along(x, (0, 1)) for x in prod]
    shapes = [square] * 3 + [(2, 2 * (order // 3), order), (2, rows, order)] + [(1, rows, order)] * (count - 1)
    sym, g0, g1, pack, own, *firsts = local_call(
        lambda *r: local_kernel(CHUNKS, *r), shapes, (a0, *prod, current_op),
        outside=(CHUNKS + 1,),
    )
    ahead = along(pack, [(j, j - 1) for j in range(2, count)])
    keep(own, 0, [0, 1])
    for to in range(1, count):
        keep(along(firsts[to - 1], (0, to)), to, [0])
    for place in range(1, count):
        after = []
        for x in before if place + 1 < count else ():
            after += local_call(lambda *r, p=place: hop_kernel(p, *r), [chunk], (x, *prod))
        if place + 1 < count:
            following = [along(x, (place, place + 1)) for x in after]
        receivers = heis_receivers(place, count)
        outs = local_call(
            lambda *r, p=place: heis_kernel(p, count, CHUNKS, *r),
            [(len(heis_slices(place, to)), rows, order) for to in receivers],
            (sym, g0, g1, *before), scratch=scratch,
        )
        for to, x in zip(receivers, outs):
            keep(x if to == place else along(x, (place, to)), to, heis_slices(place, to))
        if place + 1 < count:
            outs = local_call(
                lambda *r, p=place: ahead_kernel(p, count, CHUNKS, *r),
                [(2, rows, order)] * (place + 1), (ahead, *after), scratch=scratch,
            )
            for to, x in enumerate(outs):
                ts = [2 * place + 2, 2 * place + 3]
                keep(x if to == place else along(x, (place, to)), to, ts)
            before = following
    width = order // 2
    kept, give = local_call(lambda *r: gather_kernel(plan, *r), [(count * slices, rows, width)] * 2, arrays)
    taken = lax.ppermute(give, "col", swap)
    return pl.pallas_call(
        spectrum_kernel,
        out_shape=jax.ShapeDtypeStruct((kdev, 2, count * slices, rows, width), jnp.float32),
        in_specs=[VMEM] * 2,
        out_specs=VMEM,
        compiler_params=GRANT,
        name="spectrum",
    )(*(pltpu.with_memory_space_constraint(x, pltpu.VMEM) for x in (kept, taken)))


def is_paired(mesh, kdev, slices, order):
    count = mesh.shape["tm"]
    fits = kdev == 2 and mesh.shape["col"] == 2 and slices == 2 and count > 2
    return fits and order % 384 == 0 and order % (16 * CHUNKS) == 0 and order % (16 * count) == 0


def solution(mesh):
    def body(propagators, current_op):
        kdev, slices, order, _ = propagators.shape
        if is_paired(mesh, kdev, slices, order):
            return paired_body(propagators, current_op)
        return general_body(propagators, current_op)

    return jax.shard_map(
        body,
        mesh=mesh,
        in_specs=(P(("drive", "mom"), "tm", None, "col"), P("mom", None, None)),
        out_specs=P(("drive", "mom"), None, None, "tm", "col"),
        check_vma=False,
    )
```

```python
import math

import jax
import jax.numpy as jnp
from jax import lax
from jax.experimental import pallas as pl
from jax.experimental.pallas import tpu as pltpu
from jax.sharding import PartitionSpec as P


CHUNKS = 3
GRANT = pltpu.CompilerParams(vmem_limit_bytes=20 * 2**20)


def prefix_2(value, axis, join, neutral):
    count, mine = (lax.axis_size(axis), lax.axis_index(axis))
    pieces = lax.all_gather(value, axis)
    running = jnp.full_like(value, 0) + jnp.asarray(neutral, value.dtype)

    def turn(position, running):
        longer = join(running, pieces[position])
        return jnp.where(position < mine, longer, running)

    return lax.fori_loop(0, count - 1, turn, running)


def multiply(left, right):
    return jnp.einsum("kab,kbc->kac", left, right, precision=lax.Precision.HIGHEST)


def later_first(earlier, later):
    return multiply(later, earlier)


def chain_step(carry, unit):
    nxt = multiply(unit, carry)
    return (nxt, nxt)


def spectrum_block(block):
    length = block.shape[1]
    freq = lax.broadcasted_iota(jnp.int32, (length, length), 0)
    times = lax.broadcasted_iota(jnp.int32, (length, length), 1)
    phase = 2.0 * math.pi / length * (freq * times % length).astype(jnp.float32)
    scale = 1.0 / math.sqrt(length)
    cosine = jnp.cos(phase) * scale
    sine = -jnp.sin(phase) * scale
    real = jnp.einsum("ft,ktrc->kfrc", cosine, block, precision=lax.Precision.HIGHEST)
    imag = jnp.einsum("ft,ktrc->kfrc", sine, block, precision=lax.Precision.HIGHEST)
    return jnp.stack([real, imag], axis=1)


def general_body(propagators, current_op):
    sym = 0.5 * (current_op + jnp.swapaxes(current_op, 1, 2))
    whole = lax.all_to_all(propagators, "col", split_axis=1, concat_axis=3, tiled=True)
    kdev = whole.shape[0]
    order = whole.shape[2]
    units = jnp.moveaxis(whole, 1, 0)
    total = units[0]
    identity = jnp.broadcast_to(jnp.eye(order, dtype=jnp.float32), total.shape)
    carry_in = prefix_2(total, ("tm", "col"), later_first, identity)
    _, applied = lax.scan(chain_step, carry_in, units)
    prefix = jnp.moveaxis(applied, 0, 1)
    weighted = jnp.einsum("kab,ksbc->ksac", sym, prefix, precision=lax.Precision.HIGHEST)
    n_rows = lax.axis_size("tm")
    n_cols = lax.axis_size("col")
    row_width = order // n_rows
    col_width = order // n_cols
    slices = prefix.shape[1]
    left = prefix.reshape(kdev, slices, order, n_rows, row_width)
    right = weighted.reshape(kdev, slices, order, n_cols, col_width)
    heis = jnp.einsum("ksbir,ksbjq->ksijrq", left, right, precision=lax.Precision.HIGHEST)
    heis = heis.reshape(kdev, slices, n_rows * n_cols, row_width, col_width)
    block = lax.all_to_all(heis, ("tm", "col"), split_axis=2, concat_axis=1, tiled=True)
    return spectrum_block(block[:, :, 0])


def halves(x):
    high = x.astype(jnp.bfloat16)
    return high, (x - high.astype(jnp.float32)).astype(jnp.bfloat16)


def as_left(x):
    high, low = halves(x)
    return jnp.concatenate([high, high, low], axis=1)


def as_right(x):
    high, low = halves(x)
    return jnp.concatenate([high, low, high], axis=0)


def as_right_t(x):
    high, low = halves(x)
    return jnp.concatenate([high, low, high], axis=1)


def product(left, right):
    return jnp.dot(left, right, preferred_element_type=jnp.float32)


def product_t(left, right):
    dims = (((1,), (1,)), ((), ()))
    return lax.dot_general(left, right, dims, preferred_element_type=jnp.float32)


VMEM = pl.BlockSpec(memory_space=pltpu.VMEM)


def local_call(kernel, outs, args, scratch=(), outside=()):
    near = [
        x if i in outside else pltpu.with_memory_space_constraint(x, pltpu.VMEM)
        for i, x in enumerate(args)
    ]
    return pl.pallas_call(
        kernel,
        out_shape=[pltpu.VMEM(s, jnp.float32) for s in outs],
        in_specs=[VMEM] * len(args),
        out_specs=[VMEM] * len(outs),
        scratch_shapes=list(scratch),
        compiler_params=GRANT,
    )(*near)


def pick_kernel(own, in_ref, out_ref, sem):
    core = lax.axis_index("col")
    copy = pltpu.make_async_copy(in_ref.at[core if own else 1 - core], out_ref, sem)
    copy.start()
    copy.wait()


def start_kernel(mine_ref, got_ref, a0_ref, *refs):
    *prod_refs, a1_ref = refs
    core = lax.axis_index("col")
    part = got_ref.shape[1]
    for s, a_ref in enumerate((a0_ref, a1_ref)):
        a_ref[pl.ds(pl.multiple_of(core * part, 8), part), :] = mine_ref[s]
        a_ref[pl.ds(pl.multiple_of((1 - core) * part, 8), part), :] = got_ref[s]
    right = as_right(a1_ref[...])
    row = 0
    for p_ref in prod_refs:
        rows = p_ref.shape[0]
        p_ref[...] = product(as_left(a0_ref[row:row + rows, :]), right)
        row += rows


def packed(x):
    third = x.shape[0] // 3
    lower = jnp.concatenate([x[third:2 * third, third:], x[2 * third:, 2 * third:]], axis=1)
    return jnp.concatenate([x[:third, :], lower], axis=0)


def unpacked(x):
    third = x.shape[0] // 2
    top = x[:third, :]
    b11, b12, b22 = (x[third:, i * third:(i + 1) * third] for i in range(3))
    middle = jnp.concatenate([top[:, third:2 * third].T, b11, b12], axis=1)
    bottom = jnp.concatenate([top[:, 2 * third:].T, b12.T, b22], axis=1)
    return jnp.concatenate([top, middle, bottom], axis=0)


def local_kernel(chunks, *refs):
    a0_ref, *prod_refs, op_ref = refs[:chunks + 2]
    sym_ref, g0_ref, g1_ref, pack_ref, own_ref, *row_refs = refs[chunks + 2:]
    place = lax.axis_index("tm")
    op = op_ref[lax.axis_index("col")]
    sym = 0.5 * (op + op.T)
    sym_ref[...] = sym
    right = as_right(sym)
    a0 = a0_ref[...]
    b = jnp.concatenate([r[...] for r in prod_refs], axis=0)
    for x, g_ref in ((a0, g0_ref), (b, g1_ref)):
        g_ref[...] = product_t(as_left(product(as_left(x), right)), as_right_t(x))
    rows = own_ref.shape[1]

    @pl.when(place >= 2)
    def _():
        pack_ref[0] = packed(g0_ref[...])
        pack_ref[1] = packed(g1_ref[...])

    @pl.when(place == 0)
    def _():
        own_ref[0] = g0_ref[:rows, :]
        own_ref[1] = g1_ref[:rows, :]
        for i, row_ref in enumerate(row_refs):
            row_ref[0] = g0_ref[(i + 1) * rows:(i + 2) * rows, :]


def hop_kernel(place, in_ref, *refs):
    *prod_refs, out_ref = refs

    @pl.when(lax.axis_index("tm") == place)
    def _():
        b = jnp.concatenate([r[...] for r in prod_refs], axis=0)
        out_ref[...] = product(as_left(in_ref[...]), as_right(b))


def joined(out_ref, parts):
    row = 0
    for part in parts:
        out_ref[row:row + part.shape[0], :] = part[...]
        row += part.shape[0]


def rows_out(outs, wanted, heis, top, rows):
    for to, position in wanted.items():
        outs[to][position] = heis[to * rows - top:(to + 1) * rows - top, :]


def heis_kernel(place, count, chunks, *refs):
    sym_ref, g0_ref, g1_ref = refs[:3]
    before = refs[3:3 + chunks]
    outs, r_ref, t_ref = refs[3 + chunks:-2], refs[-2], refs[-1]
    outs = dict(zip(heis_receivers(place, count), outs))

    @pl.when(lax.axis_index("tm") == place)
    def _():
        order = sym_ref.shape[0]
        rows = order // count
        joined(r_ref, before)
        t_ref[...] = as_right_t(r_ref[...])
        for i, middle_ref in enumerate((sym_ref, g0_ref, g1_ref)):
            t = 2 * place - 1 + i
            wanted = {to: heis_slices(place, to).index(t) for to in outs if t in heis_slices(place, to)}
            top, bottom = min(wanted) * rows, (max(wanted) + 1) * rows
            weighted = product(as_left(r_ref[top:bottom, :]), as_right(middle_ref[...]))
            rows_out(outs, wanted, product_t(as_left(weighted), t_ref[...]), top, rows)


def ahead_kernel(place, count, chunks, *refs):
    pack_ref, *after = refs[:1 + chunks]
    outs, r_ref, t_ref = refs[1 + chunks:-2], refs[-2], refs[-1]

    @pl.when(lax.axis_index("tm") == place)
    def _():
        order = pack_ref.shape[2]
        rows = order // count
        joined(r_ref, after)
        t_ref[...] = as_right_t(r_ref[...])
        left = as_left(r_ref[:(place + 1) * rows, :])
        for i in range(2):
            weighted = product(left, as_right(unpacked(pack_ref[i])))
            heis = product_t(as_left(weighted), t_ref[...])
            rows_out(outs, {to: i for to in range(place + 1)}, heis, 0, rows)


def heis_slices(place, to):
    if to > place:
        return [2 * place - 1, 2 * place]
    if to == place:
        return [2 * place - 1, 2 * place, 2 * place + 1]
    return [2 * place, 2 * place + 1]


def heis_receivers(place, count):
    return [0] * (place == 1) + list(range(place, count))


def gather_kernel(chosen, *refs):
    ins, (keep_ref, send_ref) = refs[:-2], refs[-2:]
    core = lax.axis_index("col")
    width = keep_ref.shape[2]
    for to, entries in enumerate(chosen):
        @pl.when(lax.axis_index("tm") == to)
        def _(entries=entries):
            for c in range(2):
                @pl.when(core == c)
                def _(c=c):
                    for slot, (_, source, i) in enumerate(entries):
                        block = ins[source][i]
                        keep_ref[slot] = block[:, c * width:(c + 1) * width]
                        send_ref[slot] = block[:, (1 - c) * width:(2 - c) * width]


def spectrum_kernel(own, tables, *refs):
    parts, (out_ref, all_ref, done_ref, sems) = refs[:2], refs[-4:]
    place, core = lax.axis_index("tm"), lax.axis_index("col")
    length, rows, _ = all_ref.shape
    for part, table in zip(parts, tables):
        for slot in range(part.shape[0]):
            t = sum(jnp.where(place == to, ts[slot], 0) for to, ts in enumerate(table))
            all_ref[t] = part[slot]
    scale = 1.0 / math.sqrt(length)
    step = 8
    groups = 3 if rows % (3 * step) == 0 else 1
    size = rows // groups

    def cosine(n):
        return scale * math.cos(2.0 * math.pi * (n % length) / length)

    def sine(n):
        return scale * math.sin(2.0 * math.pi * (n % length) / length)

    def turn(row, carry):
        here = pl.ds(pl.multiple_of(row * step, step), step)
        values = [all_ref[t, here, :] for t in range(length)]
        for f in range(length // 2 + 1):
            real = sum(cosine(f * t) * values[t] for t in range(length))
            imag = sum(-sine(f * t) * values[t] for t in range(length))
            done_ref[0, f, here, :] = real
            done_ref[1, f, here, :] = imag
            mirrored = (length - f) % length
            if mirrored != f:
                done_ref[0, mirrored, here, :] = real
                done_ref[1, mirrored, here, :] = -imag
        return carry

    copies = []
    for g in range(groups):
        lax.fori_loop(g * size // step, (g + 1) * size // step, turn, 0)
        span = pl.ds(g * size, size)
        copy = pltpu.make_async_copy(
            done_ref.at[:, :, span, :], out_ref.at[core if own else 1 - core, :, :, span, :], sems.at[g]
        )
        copy.start()
        copies.append(copy)
    for copy in copies:
        copy.wait()


def paired_body(propagators, current_op):
    count = lax.axis_size("tm")
    flipped = jnp.swapaxes(propagators, 2, 3)
    kdev, slices, part, order = flipped.shape
    rows = order // count
    step = order // CHUNKS
    square, chunk = (order, order), (step, order)
    swap = [(0, 1), (1, 0)]
    scratch = [pltpu.VMEM(square, jnp.float32), pltpu.VMEM((order, 3 * order), jnp.bfloat16)]

    def pick(own):
        return pl.pallas_call(
            lambda *r: pick_kernel(own, *r),
            out_shape=pltpu.VMEM((slices, part, order), jnp.float32),
            in_specs=[pl.BlockSpec(memory_space=pltpu.HBM)],
            out_specs=VMEM,
            scratch_shapes=[pltpu.SemaphoreType.DMA],
            compiler_params=GRANT,
        )(pltpu.with_memory_space_constraint(flipped, pltpu.HBM))

    got = lax.ppermute(pick(False), "col", swap)
    mine = pick(True)
    a0, *prod = local_call(
        start_kernel, [square] + [chunk] * CHUNKS, (mine, got),
        scratch=[pltpu.VMEM(square, jnp.float32)],
    )

    def along(x, hop):
        return lax.ppermute(x, "tm", [hop] if isinstance(hop, tuple) else hop)

    arrays, plan = [], [[] for _ in range(count)]

    def keep(x, to, ts, rank):
        plan[to].extend((rank, t, len(arrays), i) for i, t in enumerate(ts))
        arrays.append(x)

    soon = [(1, 0), (1, count - 1)]
    before = [along(x, (0, 1)) for x in prod]
    shapes = [square] * 3 + [(2, 2 * (order // 3), order), (2, rows, order)] + [(1, rows, order)] * (count - 1)
    sym, g0, g1, pack, own, *firsts = local_call(
        lambda *r: local_kernel(CHUNKS, *r), shapes, (a0, *prod, current_op),
        outside=(CHUNKS + 1,),
    )
    ahead = along(pack, [(j, j - 1) for j in range(2, count)])
    keep(own, 0, [0, 1], 0)
    for to in range(1, count):
        keep(along(firsts[to - 1], (0, to)), to, [0], 1 if to == 1 else 5)
    for place in range(1, count):
        after = []
        for x in before if place + 1 < count else ():
            after += local_call(lambda *r, p=place: hop_kernel(p, *r), [chunk], (x, *prod))
        if place + 1 < count:
            following = [along(x, (place, place + 1)) for x in after]
        receivers = heis_receivers(place, count)
        outs = local_call(
            lambda *r, p=place: heis_kernel(p, count, CHUNKS, *r),
            [(len(heis_slices(place, to)), rows, order) for to in receivers],
            (sym, g0, g1, *before), scratch=scratch,
        )
        for to, x in zip(receivers, outs):
            ts = heis_slices(place, to)
            if to == place:
                keep(x, to, ts, 0)
            else:
                keep(along(x, (place, to)), to, ts, 1 if (place, to) in soon else 3)
        if place + 1 < count:
            outs = local_call(
                lambda *r, p=place: ahead_kernel(p, count, CHUNKS, *r),
                [(2, rows, order)] * (place + 1), (ahead, *after), scratch=scratch,
            )
            for to, x in enumerate(outs):
                ts = [2 * place + 2, 2 * place + 3]
                if to == place:
                    keep(x, to, ts, 2)
                else:
                    keep(along(x, (place, to)), to, ts, 4)
            before = following
    width = order // 2
    length = count * slices
    half = length // 2
    ordered = [[entry[1:] for entry in sorted(entries)] for entries in plan]
    kept, taken, tables = [], [], []
    for chosen in ([o[:half] for o in ordered], [o[half:] for o in ordered]):
        used = sorted({source for entries in chosen for _, source, _ in entries})
        local = [[(t, used.index(source), i) for t, source, i in entries] for entries in chosen]
        mine_part, give = local_call(
            lambda *r, c=local: gather_kernel(c, *r), [(half, rows, width)] * 2,
            [arrays[source] for source in used],
        )
        taken.append(lax.ppermute(give, "col", swap))
        kept.append(mine_part)
        tables.append([[t for t, _, _ in entries] for entries in chosen])

    def spectrum(own, parts, so_far):
        return pl.pallas_call(
            lambda *r: spectrum_kernel(own, tables, *r),
            out_shape=jax.ShapeDtypeStruct((kdev, 2, length, rows, width), jnp.float32),
            in_specs=[VMEM] * 2 + [pl.BlockSpec(memory_space=pl.ANY)] * len(so_far),
            out_specs=pl.BlockSpec(memory_space=pl.ANY),
            scratch_shapes=[
                pltpu.VMEM((length, rows, width), jnp.float32),
                pltpu.VMEM((2, length, rows, width), jnp.float32),
                pltpu.SemaphoreType.DMA((3,)),
            ],
            input_output_aliases={2: 0} if so_far else {},
            compiler_params=GRANT,
            name="spectrum",
        )(*(pltpu.with_memory_space_constraint(x, pltpu.VMEM) for x in parts), *so_far)

    return spectrum(False, taken, [spectrum(True, kept, [])])


def is_paired(mesh, kdev, slices, order):
    count = mesh.shape["tm"]
    fits = kdev == 2 and mesh.shape["col"] == 2 and slices == 2 and count > 2
    return fits and order % 384 == 0 and order % (16 * CHUNKS) == 0 and order % (16 * count) == 0


def solution(mesh):
    def body(propagators, current_op):
        kdev, slices, order, _ = propagators.shape
        if is_paired(mesh, kdev, slices, order):
            return paired_body(propagators, current_op)
        return general_body(propagators, current_op)

    return jax.shard_map(
        body,
        mesh=mesh,
        in_specs=(P(("drive", "mom"), "tm", None, "col"), P("mom", None, None)),
        out_specs=P(("drive", "mom"), None, None, "tm", "col"),
        check_vma=False,
    )
```

```python
import math

import jax
import jax.numpy as jnp
from jax import lax
from jax.experimental import pallas as pl
from jax.experimental.pallas import tpu as pltpu
from jax.sharding import PartitionSpec as P


CHUNKS = 3
GRANT = pltpu.CompilerParams(vmem_limit_bytes=20 * 2**20)


def prefix_2(value, axis, join, neutral):
    count, mine = (lax.axis_size(axis), lax.axis_index(axis))
    pieces = lax.all_gather(value, axis)
    running = jnp.full_like(value, 0) + jnp.asarray(neutral, value.dtype)

    def turn(position, running):
        longer = join(running, pieces[position])
        return jnp.where(position < mine, longer, running)

    return lax.fori_loop(0, count - 1, turn, running)


def multiply(left, right):
    return jnp.einsum("kab,kbc->kac", left, right, precision=lax.Precision.HIGHEST)


def later_first(earlier, later):
    return multiply(later, earlier)


def chain_step(carry, unit):
    nxt = multiply(unit, carry)
    return (nxt, nxt)


def spectrum_block(block):
    length = block.shape[1]
    freq = lax.broadcasted_iota(jnp.int32, (length, length), 0)
    times = lax.broadcasted_iota(jnp.int32, (length, length), 1)
    phase = 2.0 * math.pi / length * (freq * times % length).astype(jnp.float32)
    scale = 1.0 / math.sqrt(length)
    cosine = jnp.cos(phase) * scale
    sine = -jnp.sin(phase) * scale
    real = jnp.einsum("ft,ktrc->kfrc", cosine, block, precision=lax.Precision.HIGHEST)
    imag = jnp.einsum("ft,ktrc->kfrc", sine, block, precision=lax.Precision.HIGHEST)
    return jnp.stack([real, imag], axis=1)


def general_body(propagators, current_op):
    sym = 0.5 * (current_op + jnp.swapaxes(current_op, 1, 2))
    whole = lax.all_to_all(propagators, "col", split_axis=1, concat_axis=3, tiled=True)
    kdev = whole.shape[0]
    order = whole.shape[2]
    units = jnp.moveaxis(whole, 1, 0)
    total = units[0]
    identity = jnp.broadcast_to(jnp.eye(order, dtype=jnp.float32), total.shape)
    carry_in = prefix_2(total, ("tm", "col"), later_first, identity)
    _, applied = lax.scan(chain_step, carry_in, units)
    prefix = jnp.moveaxis(applied, 0, 1)
    weighted = jnp.einsum("kab,ksbc->ksac", sym, prefix, precision=lax.Precision.HIGHEST)
    n_rows = lax.axis_size("tm")
    n_cols = lax.axis_size("col")
    row_width = order // n_rows
    col_width = order // n_cols
    slices = prefix.shape[1]
    left = prefix.reshape(kdev, slices, order, n_rows, row_width)
    right = weighted.reshape(kdev, slices, order, n_cols, col_width)
    heis = jnp.einsum("ksbir,ksbjq->ksijrq", left, right, precision=lax.Precision.HIGHEST)
    heis = heis.reshape(kdev, slices, n_rows * n_cols, row_width, col_width)
    block = lax.all_to_all(heis, ("tm", "col"), split_axis=2, concat_axis=1, tiled=True)
    return spectrum_block(block[:, :, 0])


def halves(x):
    high = x.astype(jnp.bfloat16)
    return high, (x - high.astype(jnp.float32)).astype(jnp.bfloat16)


def as_left(x):
    high, low = halves(x)
    return jnp.concatenate([high, high, low], axis=1)


def as_right(x):
    high, low = halves(x)
    return jnp.concatenate([high, low, high], axis=0)


def as_right_t(x):
    high, low = halves(x)
    return jnp.concatenate([high, low, high], axis=1)


def product(left, right):
    return jnp.dot(left, right, preferred_element_type=jnp.float32)


def product_t(left, right):
    dims = (((1,), (1,)), ((), ()))
    return lax.dot_general(left, right, dims, preferred_element_type=jnp.float32)


VMEM = pl.BlockSpec(memory_space=pltpu.VMEM)


def local_call(kernel, outs, args, scratch=(), outside=()):
    near = [
        x if i in outside else pltpu.with_memory_space_constraint(x, pltpu.VMEM)
        for i, x in enumerate(args)
    ]
    return pl.pallas_call(
        kernel,
        out_shape=[pltpu.VMEM(s, jnp.float32) for s in outs],
        in_specs=[VMEM] * len(args),
        out_specs=[VMEM] * len(outs),
        scratch_shapes=list(scratch),
        compiler_params=GRANT,
    )(*near)


def pick_kernel(own, in_ref, out_ref, sem):
    core = lax.axis_index("col")
    copy = pltpu.make_async_copy(in_ref.at[core if own else 1 - core], out_ref, sem)
    copy.start()
    copy.wait()


def start_kernel(mine_ref, got_ref, a0_ref, *refs):
    *prod_refs, a1_ref = refs
    core = lax.axis_index("col")
    part = got_ref.shape[1]
    for s, a_ref in enumerate((a0_ref, a1_ref)):
        a_ref[pl.ds(pl.multiple_of(core * part, 8), part), :] = mine_ref[s]
        a_ref[pl.ds(pl.multiple_of((1 - core) * part, 8), part), :] = got_ref[s]
    right = as_right(a1_ref[...])
    row = 0
    for p_ref in prod_refs:
        rows = p_ref.shape[0]
        p_ref[...] = product(as_left(a0_ref[row:row + rows, :]), right)
        row += rows


def packed(x):
    third = x.shape[0] // 3
    lower = jnp.concatenate([x[third:2 * third, third:], x[2 * third:, 2 * third:]], axis=1)
    return jnp.concatenate([x[:third, :], lower], axis=0)


def unpacked(x):
    third = x.shape[0] // 2
    top = x[:third, :]
    b11, b12, b22 = (x[third:, i * third:(i + 1) * third] for i in range(3))
    middle = jnp.concatenate([top[:, third:2 * third].T, b11, b12], axis=1)
    bottom = jnp.concatenate([top[:, 2 * third:].T, b12.T, b22], axis=1)
    return jnp.concatenate([top, middle, bottom], axis=0)


def local_kernel(chunks, *refs):
    a0_ref, *prod_refs, op_ref = refs[:chunks + 2]
    sym_ref, g0_ref, g1_ref, pack_ref, own_ref, *row_refs = refs[chunks + 2:]
    place = lax.axis_index("tm")
    op = op_ref[lax.axis_index("col")]
    sym = 0.5 * (op + op.T)
    sym_ref[...] = sym
    right = as_right(sym)
    a0 = a0_ref[...]
    b = jnp.concatenate([r[...] for r in prod_refs], axis=0)
    for x, g_ref in ((a0, g0_ref), (b, g1_ref)):
        g_ref[...] = product_t(as_left(product(as_left(x), right)), as_right_t(x))
    rows = own_ref.shape[1]

    @pl.when(place >= 2)
    def _():
        pack_ref[0] = packed(g0_ref[...])
        pack_ref[1] = packed(g1_ref[...])

    @pl.when(place == 0)
    def _():
        own_ref[0] = g0_ref[:rows, :]
        own_ref[1] = g1_ref[:rows, :]
        for i, row_ref in enumerate(row_refs):
            row_ref[0] = g0_ref[(i + 1) * rows:(i + 2) * rows, :]


def hop_kernel(place, in_ref, *refs):
    *prod_refs, out_ref = refs

    @pl.when(lax.axis_index("tm") == place)
    def _():
        b = jnp.concatenate([r[...] for r in prod_refs], axis=0)
        out_ref[...] = product(as_left(in_ref[...]), as_right(b))


def joined(out_ref, parts):
    row = 0
    for part in parts:
        out_ref[row:row + part.shape[0], :] = part[...]
        row += part.shape[0]


def rows_out(outs, wanted, heis, top, rows):
    for to, position in wanted.items():
        outs[to][position] = heis[to * rows - top:(to + 1) * rows - top, :]


def heis_kernel(place, receivers, count, chunks, *refs):
    sym_ref, g0_ref, g1_ref = refs[:3]
    before = refs[3:3 + chunks]
    outs, r_ref, t_ref = refs[3 + chunks:-2], refs[-2], refs[-1]
    outs = dict(zip(receivers, outs))

    @pl.when(lax.axis_index("tm") == place)
    def _():
        order = sym_ref.shape[0]
        rows = order // count
        joined(r_ref, before)
        t_ref[...] = as_right_t(r_ref[...])
        for i, middle_ref in enumerate((sym_ref, g0_ref, g1_ref)):
            t = 2 * place - 1 + i
            wanted = {to: heis_slices(place, to).index(t) for to in outs if t in heis_slices(place, to)}
            if not wanted:
                continue
            top, bottom = min(wanted) * rows, (max(wanted) + 1) * rows
            weighted = product(as_left(r_ref[top:bottom, :]), as_right(middle_ref[...]))
            rows_out(outs, wanted, product_t(as_left(weighted), t_ref[...]), top, rows)


def ahead_kernel(place, count, chunks, *refs):
    pack_ref, *after = refs[:1 + chunks]
    outs, r_ref, t_ref = refs[1 + chunks:-2], refs[-2], refs[-1]

    @pl.when(lax.axis_index("tm") == place)
    def _():
        order = pack_ref.shape[2]
        rows = order // count
        joined(r_ref, after)
        t_ref[...] = as_right_t(r_ref[...])
        left = as_left(r_ref[:(place + 1) * rows, :])
        for i in range(2):
            weighted = product(left, as_right(unpacked(pack_ref[i])))
            heis = product_t(as_left(weighted), t_ref[...])
            rows_out(outs, {to: i for to in range(place + 1)}, heis, 0, rows)


def heis_slices(place, to):
    if to > place:
        return [2 * place - 1, 2 * place]
    if to == place:
        return [2 * place - 1, 2 * place, 2 * place + 1]
    return [2 * place, 2 * place + 1]


def heis_groups(place, count):
    if place == 1:
        return [[0], list(range(1, count))]
    return [list(range(place + 1, count)), [place]] if place + 1 < count else [[place]]


def gather_kernel(chosen, *refs):
    ins, (keep_ref, send_ref) = refs[:-2], refs[-2:]
    core = lax.axis_index("col")
    width = keep_ref.shape[2]
    for to, entries in enumerate(chosen):
        @pl.when(lax.axis_index("tm") == to)
        def _(entries=entries):
            for c in range(2):
                @pl.when(core == c)
                def _(c=c):
                    for slot, (_, source, i) in enumerate(entries):
                        block = ins[source][i]
                        keep_ref[slot] = block[:, c * width:(c + 1) * width]
                        send_ref[slot] = block[:, (1 - c) * width:(2 - c) * width]


def spectrum_kernel(own, tables, *refs):
    parts, (out_ref, all_ref, done_ref, sems) = refs[:2], refs[-4:]
    place, core = lax.axis_index("tm"), lax.axis_index("col")
    length, rows, _ = all_ref.shape
    for part, table in zip(parts, tables):
        for slot in range(part.shape[0]):
            t = sum(jnp.where(place == to, ts[slot], 0) for to, ts in enumerate(table))
            all_ref[t] = part[slot]
    scale = 1.0 / math.sqrt(length)
    step = 8
    groups = 3 if rows % (3 * step) == 0 else 1
    size = rows // groups

    def cosine(n):
        return scale * math.cos(2.0 * math.pi * (n % length) / length)

    def sine(n):
        return scale * math.sin(2.0 * math.pi * (n % length) / length)

    def turn(row, carry):
        here = pl.ds(pl.multiple_of(row * step, step), step)
        values = [all_ref[t, here, :] for t in range(length)]
        for f in range(length // 2 + 1):
            real = sum(cosine(f * t) * values[t] for t in range(length))
            imag = sum(-sine(f * t) * values[t] for t in range(length))
            done_ref[0, f, here, :] = real
            done_ref[1, f, here, :] = imag
            mirrored = (length - f) % length
            if mirrored != f:
                done_ref[0, mirrored, here, :] = real
                done_ref[1, mirrored, here, :] = -imag
        return carry

    copies = []
    for g in range(groups):
        lax.fori_loop(g * size // step, (g + 1) * size // step, turn, 0)
        span = pl.ds(g * size, size)
        copy = pltpu.make_async_copy(
            done_ref.at[:, :, span, :], out_ref.at[core if own else 1 - core, :, :, span, :], sems.at[g]
        )
        copy.start()
        copies.append(copy)
    for copy in copies:
        copy.wait()


def paired_body(propagators, current_op):
    count = lax.axis_size("tm")
    flipped = jnp.swapaxes(propagators, 2, 3)
    kdev, slices, part, order = flipped.shape
    rows = order // count
    step = order // CHUNKS
    square, chunk = (order, order), (step, order)
    swap = [(0, 1), (1, 0)]
    scratch = [pltpu.VMEM(square, jnp.float32), pltpu.VMEM((order, 3 * order), jnp.bfloat16)]

    def pick(own):
        return pl.pallas_call(
            lambda *r: pick_kernel(own, *r),
            out_shape=pltpu.VMEM((slices, part, order), jnp.float32),
            in_specs=[pl.BlockSpec(memory_space=pltpu.HBM)],
            out_specs=VMEM,
            scratch_shapes=[pltpu.SemaphoreType.DMA],
            compiler_params=GRANT,
        )(pltpu.with_memory_space_constraint(flipped, pltpu.HBM))

    got = lax.ppermute(pick(False), "col", swap)
    mine = pick(True)
    a0, *prod = local_call(
        start_kernel, [square] + [chunk] * CHUNKS, (mine, got),
        scratch=[pltpu.VMEM(square, jnp.float32)],
    )

    def along(x, hop):
        return lax.ppermute(x, "tm", [hop] if isinstance(hop, tuple) else hop)

    arrays, plan = [], [[] for _ in range(count)]

    def keep(x, to, ts, rank):
        plan[to].extend((rank, t, len(arrays), i) for i, t in enumerate(ts))
        arrays.append(x)

    soon = [(1, 0), (1, count - 1)]
    before = [along(x, (0, 1)) for x in prod]
    shapes = [square] * 3 + [(2, 2 * (order // 3), order), (2, rows, order)] + [(1, rows, order)] * (count - 1)
    sym, g0, g1, pack, own, *firsts = local_call(
        lambda *r: local_kernel(CHUNKS, *r), shapes, (a0, *prod, current_op),
        outside=(CHUNKS + 1,),
    )
    ahead = along(pack, [(j, j - 1) for j in range(2, count)])
    keep(own, 0, [0, 1], 0)
    for to in range(1, count):
        keep(along(firsts[to - 1], (0, to)), to, [0], 1 if to == 1 else 5)
    for place in range(1, count):
        after = []
        for x in before if place + 1 < count else ():
            after += local_call(lambda *r, p=place: hop_kernel(p, *r), [chunk], (x, *prod))
        if place + 1 < count:
            following = [along(x, (place, place + 1)) for x in after]
        for receivers in heis_groups(place, count):
            outs = local_call(
                lambda *r, p=place, w=receivers: heis_kernel(p, w, count, CHUNKS, *r),
                [(len(heis_slices(place, to)), rows, order) for to in receivers],
                (sym, g0, g1, *before), scratch=scratch,
            )
            for to, x in zip(receivers, outs):
                ts = heis_slices(place, to)
                if to == place:
                    keep(x, to, ts, 0)
                else:
                    keep(along(x, (place, to)), to, ts, 1 if (place, to) in soon else 3)
        if place + 1 < count:
            outs = local_call(
                lambda *r, p=place: ahead_kernel(p, count, CHUNKS, *r),
                [(2, rows, order)] * (place + 1), (ahead, *after), scratch=scratch,
            )
            for to, x in enumerate(outs):
                ts = [2 * place + 2, 2 * place + 3]
                if to == place:
                    keep(x, to, ts, 2)
                else:
                    keep(along(x, (place, to)), to, ts, 4)
            before = following
    width = order // 2
    length = count * slices
    half = length // 2
    ordered = [[entry[1:] for entry in sorted(entries)] for entries in plan]
    kept, taken, tables = [], [], []
    for chosen in ([o[:half] for o in ordered], [o[half:] for o in ordered]):
        used = sorted({source for entries in chosen for _, source, _ in entries})
        local = [[(t, used.index(source), i) for t, source, i in entries] for entries in chosen]
        mine_part, give = local_call(
            lambda *r, c=local: gather_kernel(c, *r), [(half, rows, width)] * 2,
            [arrays[source] for source in used],
        )
        taken.append(lax.ppermute(give, "col", swap))
        kept.append(mine_part)
        tables.append([[t for t, _, _ in entries] for entries in chosen])

    def spectrum(own, parts, so_far):
        return pl.pallas_call(
            lambda *r: spectrum_kernel(own, tables, *r),
            out_shape=jax.ShapeDtypeStruct((kdev, 2, length, rows, width), jnp.float32),
            in_specs=[VMEM] * 2 + [pl.BlockSpec(memory_space=pl.ANY)] * len(so_far),
            out_specs=pl.BlockSpec(memory_space=pl.ANY),
            scratch_shapes=[
                pltpu.VMEM((length, rows, width), jnp.float32),
                pltpu.VMEM((2, length, rows, width), jnp.float32),
                pltpu.SemaphoreType.DMA((3,)),
            ],
            input_output_aliases={2: 0} if so_far else {},
            compiler_params=GRANT,
            name="spectrum",
        )(*(pltpu.with_memory_space_constraint(x, pltpu.VMEM) for x in parts), *so_far)

    return spectrum(False, taken, [spectrum(True, kept, [])])


def is_paired(mesh, kdev, slices, order):
    count = mesh.shape["tm"]
    fits = kdev == 2 and mesh.shape["col"] == 2 and slices == 2 and count > 2
    return fits and order % 384 == 0 and order % (16 * CHUNKS) == 0 and order % (16 * count) == 0


def solution(mesh):
    def body(propagators, current_op):
        kdev, slices, order, _ = propagators.shape
        if is_paired(mesh, kdev, slices, order):
            return paired_body(propagators, current_op)
        return general_body(propagators, current_op)

    return jax.shard_map(
        body,
        mesh=mesh,
        in_specs=(P(("drive", "mom"), "tm", None, "col"), P("mom", None, None)),
        out_specs=P(("drive", "mom"), None, None, "tm", "col"),
        check_vma=False,
    )
```

```python
import math

import jax
import jax.numpy as jnp
from jax import lax
from jax.experimental import pallas as pl
from jax.experimental.pallas import tpu as pltpu
from jax.sharding import PartitionSpec as P


CHUNKS = 4
GRANT = pltpu.CompilerParams(vmem_limit_bytes=20 * 2**20)


def prefix_2(value, axis, join, neutral):
    count, mine = (lax.axis_size(axis), lax.axis_index(axis))
    pieces = lax.all_gather(value, axis)
    running = jnp.full_like(value, 0) + jnp.asarray(neutral, value.dtype)

    def turn(position, running):
        longer = join(running, pieces[position])
        return jnp.where(position < mine, longer, running)

    return lax.fori_loop(0, count - 1, turn, running)


def multiply(left, right):
    return jnp.einsum("kab,kbc->kac", left, right, precision=lax.Precision.HIGHEST)


def later_first(earlier, later):
    return multiply(later, earlier)


def chain_step(carry, unit):
    nxt = multiply(unit, carry)
    return (nxt, nxt)


def spectrum_block(block):
    length = block.shape[1]
    freq = lax.broadcasted_iota(jnp.int32, (length, length), 0)
    times = lax.broadcasted_iota(jnp.int32, (length, length), 1)
    phase = 2.0 * math.pi / length * (freq * times % length).astype(jnp.float32)
    scale = 1.0 / math.sqrt(length)
    cosine = jnp.cos(phase) * scale
    sine = -jnp.sin(phase) * scale
    real = jnp.einsum("ft,ktrc->kfrc", cosine, block, precision=lax.Precision.HIGHEST)
    imag = jnp.einsum("ft,ktrc->kfrc", sine, block, precision=lax.Precision.HIGHEST)
    return jnp.stack([real, imag], axis=1)


def general_body(propagators, current_op):
    sym = 0.5 * (current_op + jnp.swapaxes(current_op, 1, 2))
    whole = lax.all_to_all(propagators, "col", split_axis=1, concat_axis=3, tiled=True)
    kdev = whole.shape[0]
    order = whole.shape[2]
    units = jnp.moveaxis(whole, 1, 0)
    total = units[0]
    identity = jnp.broadcast_to(jnp.eye(order, dtype=jnp.float32), total.shape)
    carry_in = prefix_2(total, ("tm", "col"), later_first, identity)
    _, applied = lax.scan(chain_step, carry_in, units)
    prefix = jnp.moveaxis(applied, 0, 1)
    weighted = jnp.einsum("kab,ksbc->ksac", sym, prefix, precision=lax.Precision.HIGHEST)
    n_rows = lax.axis_size("tm")
    n_cols = lax.axis_size("col")
    row_width = order // n_rows
    col_width = order // n_cols
    slices = prefix.shape[1]
    left = prefix.reshape(kdev, slices, order, n_rows, row_width)
    right = weighted.reshape(kdev, slices, order, n_cols, col_width)
    heis = jnp.einsum("ksbir,ksbjq->ksijrq", left, right, precision=lax.Precision.HIGHEST)
    heis = heis.reshape(kdev, slices, n_rows * n_cols, row_width, col_width)
    block = lax.all_to_all(heis, ("tm", "col"), split_axis=2, concat_axis=1, tiled=True)
    return spectrum_block(block[:, :, 0])


def halves(x):
    high = x.astype(jnp.bfloat16)
    return high, (x - high.astype(jnp.float32)).astype(jnp.bfloat16)


def as_left(x):
    high, low = halves(x)
    return jnp.concatenate([high, high, low], axis=1)


def as_right(x):
    high, low = halves(x)
    return jnp.concatenate([high, low, high], axis=0)


def as_right_t(x):
    high, low = halves(x)
    return jnp.concatenate([high, low, high], axis=1)


def product(left, right):
    return jnp.dot(left, right, preferred_element_type=jnp.float32)


def product_t(left, right):
    dims = (((1,), (1,)), ((), ()))
    return lax.dot_general(left, right, dims, preferred_element_type=jnp.float32)


VMEM = pl.BlockSpec(memory_space=pltpu.VMEM)


def local_call(kernel, outs, args, scratch=(), outside=()):
    near = [
        x if i in outside else pltpu.with_memory_space_constraint(x, pltpu.VMEM)
        for i, x in enumerate(args)
    ]
    return pl.pallas_call(
        kernel,
        out_shape=[pltpu.VMEM(s, jnp.float32) for s in outs],
        in_specs=[VMEM] * len(args),
        out_specs=[VMEM] * len(outs),
        scratch_shapes=list(scratch),
        compiler_params=GRANT,
    )(*near)


def pick_kernel(own, in_ref, out_ref, sems):
    core = lax.axis_index("col")
    source = in_ref.at[core if own else 1 - core]
    slices, part, _ = out_ref.shape
    copies = []
    for s in range(slices):
        for h in range(2):
            span = pl.ds(h * (part // 2), part // 2)
            copies.append(
                pltpu.make_async_copy(source.at[s, span, :], out_ref.at[s, span, :], sems.at[2 * s + h])
            )
            copies[-1].start()
    for copy in copies:
        copy.wait()


def start_kernel(mine_ref, got_ref, a0_ref, *refs):
    *prod_refs, a1_ref = refs
    core = lax.axis_index("col")
    part = got_ref.shape[1]
    for s, a_ref in enumerate((a0_ref, a1_ref)):
        a_ref[pl.ds(pl.multiple_of(core * part, 8), part), :] = mine_ref[s]
        a_ref[pl.ds(pl.multiple_of((1 - core) * part, 8), part), :] = got_ref[s]
    right = as_right(a1_ref[...])
    row = 0
    for p_ref in prod_refs:
        rows = p_ref.shape[0]
        p_ref[...] = product(as_left(a0_ref[row:row + rows, :]), right)
        row += rows


def packed(x):
    third = x.shape[0] // 3
    lower = jnp.concatenate([x[third:2 * third, third:], x[2 * third:, 2 * third:]], axis=1)
    return jnp.concatenate([x[:third, :], lower], axis=0)


def unpacked(x):
    third = x.shape[0] // 2
    top = x[:third, :]
    b11, b12, b22 = (x[third:, i * third:(i + 1) * third] for i in range(3))
    middle = jnp.concatenate([top[:, third:2 * third].T, b11, b12], axis=1)
    bottom = jnp.concatenate([top[:, 2 * third:].T, b12.T, b22], axis=1)
    return jnp.concatenate([top, middle, bottom], axis=0)


def local_kernel(chunks, *refs):
    a0_ref, *prod_refs, op_ref = refs[:chunks + 2]
    sym_ref, g0_ref, g1_ref, pack_ref, own_ref, *row_refs = refs[chunks + 2:]
    place = lax.axis_index("tm")
    op = op_ref[lax.axis_index("col")]
    sym = 0.5 * (op + op.T)
    sym_ref[...] = sym
    right = as_right(sym)
    a0 = a0_ref[...]
    b = jnp.concatenate([r[...] for r in prod_refs], axis=0)
    for x, g_ref in ((a0, g0_ref), (b, g1_ref)):
        g_ref[...] = product_t(as_left(product(as_left(x), right)), as_right_t(x))
    rows = own_ref.shape[1]

    @pl.when(place >= 2)
    def _():
        pack_ref[0] = packed(g0_ref[...])
        pack_ref[1] = packed(g1_ref[...])

    @pl.when(place == 0)
    def _():
        own_ref[0] = g0_ref[:rows, :]
        own_ref[1] = g1_ref[:rows, :]
        for i, row_ref in enumerate(row_refs):
            row_ref[0] = g0_ref[(i + 1) * rows:(i + 2) * rows, :]


def hop_kernel(place, in_ref, *refs):
    *prod_refs, out_ref = refs

    @pl.when(lax.axis_index("tm") == place)
    def _():
        b = jnp.concatenate([r[...] for r in prod_refs], axis=0)
        out_ref[...] = product(as_left(in_ref[...]), as_right(b))


def joined(out_ref, parts):
    row = 0
    for part in parts:
        out_ref[row:row + part.shape[0], :] = part[...]
        row += part.shape[0]


def rows_out(outs, wanted, heis, top, rows):
    for to, position in wanted.items():
        outs[to][position] = heis[to * rows - top:(to + 1) * rows - top, :]


def heis_kernel(place, receivers, count, chunks, *refs):
    sym_ref, g0_ref, g1_ref = refs[:3]
    before = refs[3:3 + chunks]
    outs, r_ref, t_ref = refs[3 + chunks:-2], refs[-2], refs[-1]
    outs = dict(zip(receivers, outs))

    @pl.when(lax.axis_index("tm") == place)
    def _():
        order = sym_ref.shape[0]
        rows = order // count
        joined(r_ref, before)
        t_ref[...] = as_right_t(r_ref[...])
        for i, middle_ref in enumerate((sym_ref, g0_ref, g1_ref)):
            t = 2 * place - 1 + i
            wanted = {to: heis_slices(place, to).index(t) for to in outs if t in heis_slices(place, to)}
            if not wanted:
                continue
            top, bottom = min(wanted) * rows, (max(wanted) + 1) * rows
            weighted = product(as_left(r_ref[top:bottom, :]), as_right(middle_ref[...]))
            rows_out(outs, wanted, product_t(as_left(weighted), t_ref[...]), top, rows)


def ahead_kernel(place, count, chunks, *refs):
    pack_ref, *after = refs[:1 + chunks]
    outs, r_ref, t_ref = refs[1 + chunks:-2], refs[-2], refs[-1]

    @pl.when(lax.axis_index("tm") == place)
    def _():
        order = pack_ref.shape[2]
        rows = order // count
        joined(r_ref, after)
        t_ref[...] = as_right_t(r_ref[...])
        left = as_left(r_ref[:(place + 1) * rows, :])
        for i in range(2):
            weighted = product(left, as_right(unpacked(pack_ref[i])))
            heis = product_t(as_left(weighted), t_ref[...])
            rows_out(outs, {to: i for to in range(place + 1)}, heis, 0, rows)


def heis_slices(place, to):
    if to > place:
        return [2 * place - 1, 2 * place]
    if to == place:
        return [2 * place - 1, 2 * place, 2 * place + 1]
    return [2 * place, 2 * place + 1]


def heis_groups(place, count):
    if place == 1:
        return [[0], list(range(1, count))]
    return [list(range(place + 1, count)), [place]] if place + 1 < count else [[place]]


def gather_kernel(chosen, *refs):
    ins, (keep_ref, send_ref) = refs[:-2], refs[-2:]
    core = lax.axis_index("col")
    width = keep_ref.shape[2]
    for to, entries in enumerate(chosen):
        @pl.when(lax.axis_index("tm") == to)
        def _(entries=entries):
            for c in range(2):
                @pl.when(core == c)
                def _(c=c):
                    for slot, (_, source, i) in enumerate(entries):
                        block = ins[source][i]
                        keep_ref[slot] = block[:, c * width:(c + 1) * width]
                        send_ref[slot] = block[:, (1 - c) * width:(2 - c) * width]


def spectrum_kernel(own, tables, *refs):
    parts, (out_ref, all_ref, done_ref, sems) = refs[:2], refs[-4:]
    place, core = lax.axis_index("tm"), lax.axis_index("col")
    length, rows, _ = all_ref.shape
    for part, table in zip(parts, tables):
        for slot in range(part.shape[0]):
            t = sum(jnp.where(place == to, ts[slot], 0) for to, ts in enumerate(table))
            all_ref[t] = part[slot]
    scale = 1.0 / math.sqrt(length)
    step = 8
    groups = 3 if rows % (3 * step) == 0 else 1
    size = rows // groups

    def cosine(n):
        return scale * math.cos(2.0 * math.pi * (n % length) / length)

    def sine(n):
        return scale * math.sin(2.0 * math.pi * (n % length) / length)

    def turn(row, carry):
        here = pl.ds(pl.multiple_of(row * step, step), step)
        values = [all_ref[t, here, :] for t in range(length)]
        for f in range(length // 2 + 1):
            real = sum(cosine(f * t) * values[t] for t in range(length))
            imag = sum(-sine(f * t) * values[t] for t in range(length))
            done_ref[0, f, here, :] = real
            done_ref[1, f, here, :] = imag
            mirrored = (length - f) % length
            if mirrored != f:
                done_ref[0, mirrored, here, :] = real
                done_ref[1, mirrored, here, :] = -imag
        return carry

    copies = []
    for g in range(groups):
        lax.fori_loop(g * size // step, (g + 1) * size // step, turn, 0)
        span = pl.ds(g * size, size)
        copy = pltpu.make_async_copy(
            done_ref.at[:, :, span, :], out_ref.at[core if own else 1 - core, :, :, span, :], sems.at[g]
        )
        copy.start()
        copies.append(copy)
    for copy in copies:
        copy.wait()


def paired_body(propagators, current_op):
    count = lax.axis_size("tm")
    flipped = jnp.swapaxes(propagators, 2, 3)
    kdev, slices, part, order = flipped.shape
    rows = order // count
    step = order // CHUNKS
    square, chunk = (order, order), (step, order)
    swap = [(0, 1), (1, 0)]
    scratch = [pltpu.VMEM(square, jnp.float32), pltpu.VMEM((order, 3 * order), jnp.bfloat16)]

    def pick(own):
        return pl.pallas_call(
            lambda *r: pick_kernel(own, *r),
            out_shape=pltpu.VMEM((slices, part, order), jnp.float32),
            in_specs=[pl.BlockSpec(memory_space=pltpu.HBM)],
            out_specs=VMEM,
            scratch_shapes=[pltpu.SemaphoreType.DMA((2 * slices,))],
            compiler_params=GRANT,
        )(pltpu.with_memory_space_constraint(flipped, pltpu.HBM))

    got = lax.ppermute(pick(False), "col", swap)
    mine = pick(True)
    a0, *prod = local_call(
        start_kernel, [square] + [chunk] * CHUNKS, (mine, got),
        scratch=[pltpu.VMEM(square, jnp.float32)],
    )

    def along(x, hop):
        return lax.ppermute(x, "tm", [hop] if isinstance(hop, tuple) else hop)

    arrays, plan = [], [[] for _ in range(count)]

    def keep(x, to, ts, rank):
        plan[to].extend((rank, t, len(arrays), i) for i, t in enumerate(ts))
        arrays.append(x)

    soon = [(1, 0), (1, count - 1)]
    before = [along(x, (0, 1)) for x in prod]
    shapes = [square] * 3 + [(2, 2 * (order // 3), order), (2, rows, order)] + [(1, rows, order)] * (count - 1)
    sym, g0, g1, pack, own, *firsts = local_call(
        lambda *r: local_kernel(CHUNKS, *r), shapes, (a0, *prod, current_op),
        outside=(CHUNKS + 1,),
    )
    ahead = along(pack, [(j, j - 1) for j in range(2, count)])
    keep(own, 0, [0, 1], 0)
    for to in range(1, count):
        keep(along(firsts[to - 1], (0, to)), to, [0], 1 if to == 1 else 5)
    for place in range(1, count):
        after = []
        for x in before if place + 1 < count else ():
            after += local_call(lambda *r, p=place: hop_kernel(p, *r), [chunk], (x, *prod))
        if place + 1 < count:
            following = [along(x, (place, place + 1)) for x in after]
        for receivers in heis_groups(place, count):
            outs = local_call(
                lambda *r, p=place, w=receivers: heis_kernel(p, w, count, CHUNKS, *r),
                [(len(heis_slices(place, to)), rows, order) for to in receivers],
                (sym, g0, g1, *before), scratch=scratch,
            )
            for to, x in zip(receivers, outs):
                ts = heis_slices(place, to)
                if to == place:
                    keep(x, to, ts, 0)
                else:
                    keep(along(x, (place, to)), to, ts, 1 if (place, to) in soon else 3)
        if place + 1 < count:
            outs = local_call(
                lambda *r, p=place: ahead_kernel(p, count, CHUNKS, *r),
                [(2, rows, order)] * (place + 1), (ahead, *after), scratch=scratch,
            )
            for to, x in enumerate(outs):
                ts = [2 * place + 2, 2 * place + 3]
                if to == place:
                    keep(x, to, ts, 2)
                else:
                    keep(along(x, (place, to)), to, ts, 4)
            before = following
    width = order // 2
    length = count * slices
    half = length // 2
    ordered = [[entry[1:] for entry in sorted(entries)] for entries in plan]
    kept, taken, tables = [], [], []
    for chosen in ([o[:half] for o in ordered], [o[half:] for o in ordered]):
        used = sorted({source for entries in chosen for _, source, _ in entries})
        local = [[(t, used.index(source), i) for t, source, i in entries] for entries in chosen]
        mine_part, give = local_call(
            lambda *r, c=local: gather_kernel(c, *r), [(half, rows, width)] * 2,
            [arrays[source] for source in used],
        )
        taken.append(lax.ppermute(give, "col", swap))
        kept.append(mine_part)
        tables.append([[t for t, _, _ in entries] for entries in chosen])

    def spectrum(own, parts, so_far):
        return pl.pallas_call(
            lambda *r: spectrum_kernel(own, tables, *r),
            out_shape=jax.ShapeDtypeStruct((kdev, 2, length, rows, width), jnp.float32),
            in_specs=[VMEM] * 2 + [pl.BlockSpec(memory_space=pl.ANY)] * len(so_far),
            out_specs=pl.BlockSpec(memory_space=pl.ANY),
            scratch_shapes=[
                pltpu.VMEM((length, rows, width), jnp.float32),
                pltpu.VMEM((2, length, rows, width), jnp.float32),
                pltpu.SemaphoreType.DMA((3,)),
            ],
            input_output_aliases={2: 0} if so_far else {},
            compiler_params=GRANT,
            name="spectrum",
        )(*(pltpu.with_memory_space_constraint(x, pltpu.VMEM) for x in parts), *so_far)

    return spectrum(False, taken, [spectrum(True, kept, [])])


def is_paired(mesh, kdev, slices, order):
    count = mesh.shape["tm"]
    fits = kdev == 2 and mesh.shape["col"] == 2 and slices == 2 and count > 2
    return fits and order % 384 == 0 and order % (16 * CHUNKS) == 0 and order % (16 * count) == 0


def solution(mesh):
    def body(propagators, current_op):
        kdev, slices, order, _ = propagators.shape
        if is_paired(mesh, kdev, slices, order):
            return paired_body(propagators, current_op)
        return general_body(propagators, current_op)

    return jax.shard_map(
        body,
        mesh=mesh,
        in_specs=(P(("drive", "mom"), "tm", None, "col"), P("mom", None, None)),
        out_specs=P(("drive", "mom"), None, None, "tm", "col"),
        check_vma=False,
    )
```

```python
import math

import jax
import jax.numpy as jnp
from jax import lax
from jax.experimental import pallas as pl
from jax.experimental.pallas import tpu as pltpu
from jax.sharding import PartitionSpec as P


CHUNKS = 3
GRANT = pltpu.CompilerParams(vmem_limit_bytes=20 * 2**20)


def prefix_2(value, axis, join, neutral):
    count, mine = (lax.axis_size(axis), lax.axis_index(axis))
    pieces = lax.all_gather(value, axis)
    running = jnp.full_like(value, 0) + jnp.asarray(neutral, value.dtype)

    def turn(position, running):
        longer = join(running, pieces[position])
        return jnp.where(position < mine, longer, running)

    return lax.fori_loop(0, count - 1, turn, running)


def multiply(left, right):
    return jnp.einsum("kab,kbc->kac", left, right, precision=lax.Precision.HIGHEST)


def later_first(earlier, later):
    return multiply(later, earlier)


def chain_step(carry, unit):
    nxt = multiply(unit, carry)
    return (nxt, nxt)


def spectrum_block(block):
    length = block.shape[1]
    freq = lax.broadcasted_iota(jnp.int32, (length, length), 0)
    times = lax.broadcasted_iota(jnp.int32, (length, length), 1)
    phase = 2.0 * math.pi / length * (freq * times % length).astype(jnp.float32)
    scale = 1.0 / math.sqrt(length)
    cosine = jnp.cos(phase) * scale
    sine = -jnp.sin(phase) * scale
    real = jnp.einsum("ft,ktrc->kfrc", cosine, block, precision=lax.Precision.HIGHEST)
    imag = jnp.einsum("ft,ktrc->kfrc", sine, block, precision=lax.Precision.HIGHEST)
    return jnp.stack([real, imag], axis=1)


def general_body(propagators, current_op):
    sym = 0.5 * (current_op + jnp.swapaxes(current_op, 1, 2))
    whole = lax.all_to_all(propagators, "col", split_axis=1, concat_axis=3, tiled=True)
    kdev = whole.shape[0]
    order = whole.shape[2]
    units = jnp.moveaxis(whole, 1, 0)
    total = units[0]
    identity = jnp.broadcast_to(jnp.eye(order, dtype=jnp.float32), total.shape)
    carry_in = prefix_2(total, ("tm", "col"), later_first, identity)
    _, applied = lax.scan(chain_step, carry_in, units)
    prefix = jnp.moveaxis(applied, 0, 1)
    weighted = jnp.einsum("kab,ksbc->ksac", sym, prefix, precision=lax.Precision.HIGHEST)
    n_rows = lax.axis_size("tm")
    n_cols = lax.axis_size("col")
    row_width = order // n_rows
    col_width = order // n_cols
    slices = prefix.shape[1]
    left = prefix.reshape(kdev, slices, order, n_rows, row_width)
    right = weighted.reshape(kdev, slices, order, n_cols, col_width)
    heis = jnp.einsum("ksbir,ksbjq->ksijrq", left, right, precision=lax.Precision.HIGHEST)
    heis = heis.reshape(kdev, slices, n_rows * n_cols, row_width, col_width)
    block = lax.all_to_all(heis, ("tm", "col"), split_axis=2, concat_axis=1, tiled=True)
    return spectrum_block(block[:, :, 0])


def halves(x):
    high = x.astype(jnp.bfloat16)
    return high, (x - high.astype(jnp.float32)).astype(jnp.bfloat16)


def as_left(x):
    high, low = halves(x)
    return jnp.concatenate([high, high, low], axis=1)


def as_right(x):
    high, low = halves(x)
    return jnp.concatenate([high, low, high], axis=0)


def as_right_t(x):
    high, low = halves(x)
    return jnp.concatenate([high, low, high], axis=1)


def product(left, right):
    return jnp.dot(left, right, preferred_element_type=jnp.float32)


def product_t(left, right):
    dims = (((1,), (1,)), ((), ()))
    return lax.dot_general(left, right, dims, preferred_element_type=jnp.float32)


VMEM = pl.BlockSpec(memory_space=pltpu.VMEM)


def local_call(kernel, outs, args, scratch=(), outside=()):
    near = [
        x if i in outside else pltpu.with_memory_space_constraint(x, pltpu.VMEM)
        for i, x in enumerate(args)
    ]
    return pl.pallas_call(
        kernel,
        out_shape=[pltpu.VMEM(s, jnp.float32) for s in outs],
        in_specs=[VMEM] * len(args),
        out_specs=[VMEM] * len(outs),
        scratch_shapes=list(scratch),
        compiler_params=GRANT,
    )(*near)


def pick_kernel(own, in_ref, out_ref, sems):
    core = lax.axis_index("col")
    source = in_ref.at[core if own else 1 - core]
    slices, part, _ = out_ref.shape
    copies = []
    for s in range(slices):
        for h in range(2):
            span = pl.ds(h * (part // 2), part // 2)
            copies.append(
                pltpu.make_async_copy(source.at[s, span, :], out_ref.at[s, span, :], sems.at[2 * s + h])
            )
            copies[-1].start()
    for copy in copies:
        copy.wait()


def start_kernel(mine_ref, got_ref, a0_ref, *refs):
    *prod_refs, a1_ref = refs
    core = lax.axis_index("col")
    part = got_ref.shape[1]
    for s, a_ref in enumerate((a0_ref, a1_ref)):
        a_ref[pl.ds(pl.multiple_of(core * part, 8), part), :] = mine_ref[s]
        a_ref[pl.ds(pl.multiple_of((1 - core) * part, 8), part), :] = got_ref[s]
    right = as_right(a1_ref[...])
    row = 0
    for p_ref in prod_refs:
        rows = p_ref.shape[0]
        p_ref[...] = product(as_left(a0_ref[row:row + rows, :]), right)
        row += rows


def packed(x):
    third = x.shape[0] // 3
    lower = jnp.concatenate([x[third:2 * third, third:], x[2 * third:, 2 * third:]], axis=1)
    return jnp.concatenate([x[:third, :], lower], axis=0)


def unpacked(x):
    third = x.shape[0] // 2
    top = x[:third, :]
    b11, b12, b22 = (x[third:, i * third:(i + 1) * third] for i in range(3))
    middle = jnp.concatenate([top[:, third:2 * third].T, b11, b12], axis=1)
    bottom = jnp.concatenate([top[:, 2 * third:].T, b12.T, b22], axis=1)
    return jnp.concatenate([top, middle, bottom], axis=0)


def local_kernel(chunks, *refs):
    a0_ref, *prod_refs, op_ref = refs[:chunks + 2]
    sym_ref, g0_ref, g1_ref, b_ref, pack_ref, own_ref, *row_refs = refs[chunks + 2:]
    place = lax.axis_index("tm")
    op = op_ref[lax.axis_index("col")]
    sym = 0.5 * (op + op.T)
    sym_ref[...] = sym
    right = as_right(sym)
    a0 = a0_ref[...]
    b = jnp.concatenate([r[...] for r in prod_refs], axis=0)
    b_ref[...] = b
    for x, g_ref in ((a0, g0_ref), (b, g1_ref)):
        g_ref[...] = product_t(as_left(product(as_left(x), right)), as_right_t(x))
    rows = own_ref.shape[1]

    @pl.when(place >= 2)
    def _():
        pack_ref[0] = packed(g0_ref[...])
        pack_ref[1] = packed(g1_ref[...])

    @pl.when(place == 0)
    def _():
        own_ref[0] = g0_ref[:rows, :]
        own_ref[1] = g1_ref[:rows, :]
        for i, row_ref in enumerate(row_refs):
            row_ref[0] = g0_ref[(i + 1) * rows:(i + 2) * rows, :]


def hop_kernel(place, in_ref, *refs):
    *prod_refs, out_ref = refs

    @pl.when(lax.axis_index("tm") == place)
    def _():
        b = jnp.concatenate([r[...] for r in prod_refs], axis=0)
        out_ref[...] = product(as_left(in_ref[...]), as_right(b))


def joined(out_ref, parts):
    row = 0
    for part in parts:
        out_ref[row:row + part.shape[0], :] = part[...]
        row += part.shape[0]


def rows_out(outs, wanted, heis, top, rows):
    for to, position in wanted.items():
        outs[to][position] = heis[to * rows - top:(to + 1) * rows - top, :]


def heis_kernel(place, receivers, count, chunks, *refs):
    sym_ref, g0_ref, g1_ref = refs[:3]
    before = refs[3:3 + chunks]
    outs, r_ref, t_ref = refs[3 + chunks:-2], refs[-2], refs[-1]
    outs = dict(zip(receivers, outs))

    @pl.when(lax.axis_index("tm") == place)
    def _():
        order = sym_ref.shape[0]
        rows = order // count
        joined(r_ref, before)
        t_ref[...] = as_right_t(r_ref[...])
        for i, middle_ref in enumerate((sym_ref, g0_ref, g1_ref)):
            t = 2 * place - 1 + i
            known = {to: heis_slices(place, to, count) for to in outs}
            wanted = {to: ts.index(t) for to, ts in known.items() if t in ts}
            if not wanted:
                continue
            top, bottom = min(wanted) * rows, (max(wanted) + 1) * rows
            weighted = product(as_left(r_ref[top:bottom, :]), as_right(middle_ref[...]))
            rows_out(outs, wanted, product_t(as_left(weighted), t_ref[...]), top, rows)


def last_kernel(count, chunks, *refs):
    sym_ref, g0_ref, g1_ref, step_ref = refs[:4]
    before = refs[4:4 + chunks]
    out_ref, r_ref, t_ref = refs[4 + chunks:]

    @pl.when(lax.axis_index("tm") == count - 1)
    def _():
        rows = out_ref.shape[1]
        top = (count - 1) * rows

        def own_rows(position, middle_ref):
            weighted = product(as_left(r_ref[top:, :]), as_right(middle_ref[...]))
            out_ref[position] = product_t(as_left(weighted), t_ref[...])

        joined(r_ref, before)
        t_ref[...] = as_right_t(r_ref[...])
        own_rows(0, sym_ref)
        r_ref[...] = product(as_left(r_ref[...]), as_right(step_ref[...]))
        t_ref[...] = as_right_t(r_ref[...])
        for i, middle_ref in enumerate((sym_ref, g0_ref, g1_ref)):
            own_rows(1 + i, middle_ref)


def ahead_kernel(place, count, chunks, *refs):
    pack_ref, *after = refs[:1 + chunks]
    outs, r_ref, t_ref = refs[1 + chunks:-2], refs[-2], refs[-1]

    @pl.when(lax.axis_index("tm") == place)
    def _():
        order = pack_ref.shape[2]
        rows = order // count
        joined(r_ref, after)
        t_ref[...] = as_right_t(r_ref[...])
        left = as_left(r_ref[:(place + 1) * rows, :])
        for i in range(2):
            weighted = product(left, as_right(unpacked(pack_ref[i])))
            heis = product_t(as_left(weighted), t_ref[...])
            rows_out(outs, {to: i for to in range(place + 1)}, heis, 0, rows)


def heis_slices(place, to, count):
    if to > place:
        return [2 * place] if place == count - 2 else [2 * place - 1, 2 * place]
    if to == place:
        return [2 * place - 3] * (place == count - 1) + [2 * place - 1, 2 * place, 2 * place + 1]
    return [2 * place, 2 * place + 1]


def heis_groups(place, count):
    if place == 1:
        return [[0], list(range(1, count))]
    return [list(range(place + 1, count)), [place]] if place + 1 < count else []


def gather_kernel(chosen, *refs):
    ins, (keep_ref, send_ref) = refs[:-2], refs[-2:]
    core = lax.axis_index("col")
    width = keep_ref.shape[2]
    for to, entries in enumerate(chosen):
        @pl.when(lax.axis_index("tm") == to)
        def _(entries=entries):
            for c in range(2):
                @pl.when(core == c)
                def _(c=c):
                    for slot, (_, source, i) in enumerate(entries):
                        block = ins[source][i]
                        keep_ref[slot] = block[:, c * width:(c + 1) * width]
                        send_ref[slot] = block[:, (1 - c) * width:(2 - c) * width]


def spectrum_kernel(own, tables, *refs):
    parts, (out_ref, all_ref, done_ref, sems) = refs[:2], refs[-4:]
    place, core = lax.axis_index("tm"), lax.axis_index("col")
    length, rows, _ = all_ref.shape
    for part, table in zip(parts, tables):
        for slot in range(part.shape[0]):
            t = sum(jnp.where(place == to, ts[slot], 0) for to, ts in enumerate(table))
            all_ref[t] = part[slot]
    scale = 1.0 / math.sqrt(length)
    step = 8
    groups = 3 if rows % (3 * step) == 0 else 1
    size = rows // groups

    def cosine(n):
        return scale * math.cos(2.0 * math.pi * (n % length) / length)

    def sine(n):
        return scale * math.sin(2.0 * math.pi * (n % length) / length)

    def turn(row, carry):
        here = pl.ds(pl.multiple_of(row * step, step), step)
        values = [all_ref[t, here, :] for t in range(length)]
        for f in range(length // 2 + 1):
            real = sum(cosine(f * t) * values[t] for t in range(length))
            imag = sum(-sine(f * t) * values[t] for t in range(length))
            done_ref[0, f, here, :] = real
            done_ref[1, f, here, :] = imag
            mirrored = (length - f) % length
            if mirrored != f:
                done_ref[0, mirrored, here, :] = real
                done_ref[1, mirrored, here, :] = -imag
        return carry

    copies = []
    for g in range(groups):
        lax.fori_loop(g * size // step, (g + 1) * size // step, turn, 0)
        span = pl.ds(g * size, size)
        copy = pltpu.make_async_copy(
            done_ref.at[:, :, span, :], out_ref.at[core if own else 1 - core, :, :, span, :], sems.at[g]
        )
        copy.start()
        copies.append(copy)
    for copy in copies:
        copy.wait()


def paired_body(propagators, current_op):
    count = lax.axis_size("tm")
    flipped = jnp.swapaxes(propagators, 2, 3)
    kdev, slices, part, order = flipped.shape
    rows = order // count
    step = order // CHUNKS
    square, chunk = (order, order), (step, order)
    swap = [(0, 1), (1, 0)]
    scratch = [pltpu.VMEM(square, jnp.float32), pltpu.VMEM((order, 3 * order), jnp.bfloat16)]

    def pick(own):
        return pl.pallas_call(
            lambda *r: pick_kernel(own, *r),
            out_shape=pltpu.VMEM((slices, part, order), jnp.float32),
            in_specs=[pl.BlockSpec(memory_space=pltpu.HBM)],
            out_specs=VMEM,
            scratch_shapes=[pltpu.SemaphoreType.DMA((2 * slices,))],
            compiler_params=GRANT,
        )(pltpu.with_memory_space_constraint(flipped, pltpu.HBM))

    got = lax.ppermute(pick(False), "col", swap)
    mine = pick(True)
    a0, *prod = local_call(
        start_kernel, [square] + [chunk] * CHUNKS, (mine, got),
        scratch=[pltpu.VMEM(square, jnp.float32)],
    )

    def along(x, hop):
        return lax.ppermute(x, "tm", [hop] if isinstance(hop, tuple) else hop)

    arrays, plan = [], [[] for _ in range(count)]

    def keep(x, to, ts, rank):
        plan[to].extend((rank, t, len(arrays), i) for i, t in enumerate(ts))
        arrays.append(x)

    soon = [(1, 0)]
    before = [along(x, (0, 1)) for x in prod]
    shapes = [square] * 4 + [(2, 2 * (order // 3), order), (2, rows, order)] + [(1, rows, order)] * (count - 1)
    sym, g0, g1, whole, pack, own, *firsts = local_call(
        lambda *r: local_kernel(CHUNKS, *r), shapes, (a0, *prod, current_op),
        outside=(CHUNKS + 1,),
    )
    last_step = along(whole, (count - 2, count - 1))
    ahead = along(pack, [(j, j - 1) for j in range(2, count)])
    keep(own, 0, [0, 1], 0)
    for to in range(1, count):
        keep(along(firsts[to - 1], (0, to)), to, [0], 1 if to == 1 else 5)
    for place in range(1, count - 1):
        after = []
        for x in before:
            after += local_call(lambda *r, p=place: hop_kernel(p, *r), [chunk], (x, *prod))
        passed = after if place < count - 2 else before
        following = [along(x, (place, place + 1)) for x in passed]
        for receivers in heis_groups(place, count):
            outs = local_call(
                lambda *r, p=place, w=receivers: heis_kernel(p, w, count, CHUNKS, *r),
                [(len(heis_slices(place, to, count)), rows, order) for to in receivers],
                (sym, g0, g1, *before), scratch=scratch,
            )
            for to, x in zip(receivers, outs):
                ts = heis_slices(place, to, count)
                if to == place:
                    keep(x, to, ts, 0)
                else:
                    keep(along(x, (place, to)), to, ts, 1 if (place, to) in soon else 3)
        outs = local_call(
            lambda *r, p=place: ahead_kernel(p, count, CHUNKS, *r),
            [(2, rows, order)] * (place + 1), (ahead, *after), scratch=scratch,
        )
        for to, x in enumerate(outs):
            ts = [2 * place + 2, 2 * place + 3]
            if to == place:
                keep(x, to, ts, 2)
            else:
                keep(along(x, (place, to)), to, ts, 4)
        before = following
    last_slices = heis_slices(count - 1, count - 1, count)
    outs = local_call(
        lambda *r: last_kernel(count, CHUNKS, *r), [(len(last_slices), rows, order)],
        (sym, g0, g1, last_step, *before), scratch=scratch,
    )
    keep(outs[0], count - 1, last_slices, 0)
    width = order // 2
    length = count * slices
    half = length // 2
    ordered = [[entry[1:] for entry in sorted(entries)] for entries in plan]
    kept, taken, tables = [], [], []
    for chosen in ([o[:half] for o in ordered], [o[half:] for o in ordered]):
        used = sorted({source for entries in chosen for _, source, _ in entries})
        local = [[(t, used.index(source), i) for t, source, i in entries] for entries in chosen]
        mine_part, give = local_call(
            lambda *r, c=local: gather_kernel(c, *r), [(half, rows, width)] * 2,
            [arrays[source] for source in used],
        )
        taken.append(lax.ppermute(give, "col", swap))
        kept.append(mine_part)
        tables.append([[t for t, _, _ in entries] for entries in chosen])

    def spectrum(own, parts, so_far):
        return pl.pallas_call(
            lambda *r: spectrum_kernel(own, tables, *r),
            out_shape=jax.ShapeDtypeStruct((kdev, 2, length, rows, width), jnp.float32),
            in_specs=[VMEM] * 2 + [pl.BlockSpec(memory_space=pl.ANY)] * len(so_far),
            out_specs=pl.BlockSpec(memory_space=pl.ANY),
            scratch_shapes=[
                pltpu.VMEM((length, rows, width), jnp.float32),
                pltpu.VMEM((2, length, rows, width), jnp.float32),
                pltpu.SemaphoreType.DMA((3,)),
            ],
            input_output_aliases={2: 0} if so_far else {},
            compiler_params=GRANT,
            name="spectrum",
        )(*(pltpu.with_memory_space_constraint(x, pltpu.VMEM) for x in parts), *so_far)

    return spectrum(False, taken, [spectrum(True, kept, [])])


def is_paired(mesh, kdev, slices, order):
    count = mesh.shape["tm"]
    fits = kdev == 2 and mesh.shape["col"] == 2 and slices == 2 and count > 2
    return fits and order % 384 == 0 and order % (16 * CHUNKS) == 0 and order % (16 * count) == 0


def solution(mesh):
    def body(propagators, current_op):
        kdev, slices, order, _ = propagators.shape
        if is_paired(mesh, kdev, slices, order):
            return paired_body(propagators, current_op)
        return general_body(propagators, current_op)

    return jax.shard_map(
        body,
        mesh=mesh,
        in_specs=(P(("drive", "mom"), "tm", None, "col"), P("mom", None, None)),
        out_specs=P(("drive", "mom"), None, None, "tm", "col"),
        check_vma=False,
    )
```

```python
import math

import jax
import jax.numpy as jnp
from jax import lax
from jax.experimental import pallas as pl
from jax.experimental.pallas import tpu as pltpu
from jax.sharding import PartitionSpec as P


CHUNKS = 3
GRANT = pltpu.CompilerParams(vmem_limit_bytes=20 * 2**20)


def prefix_2(value, axis, join, neutral):
    count, mine = (lax.axis_size(axis), lax.axis_index(axis))
    pieces = lax.all_gather(value, axis)
    running = jnp.full_like(value, 0) + jnp.asarray(neutral, value.dtype)

    def turn(position, running):
        longer = join(running, pieces[position])
        return jnp.where(position < mine, longer, running)

    return lax.fori_loop(0, count - 1, turn, running)


def multiply(left, right):
    return jnp.einsum("kab,kbc->kac", left, right, precision=lax.Precision.HIGHEST)


def later_first(earlier, later):
    return multiply(later, earlier)


def chain_step(carry, unit):
    nxt = multiply(unit, carry)
    return (nxt, nxt)


def spectrum_block(block):
    length = block.shape[1]
    freq = lax.broadcasted_iota(jnp.int32, (length, length), 0)
    times = lax.broadcasted_iota(jnp.int32, (length, length), 1)
    phase = 2.0 * math.pi / length * (freq * times % length).astype(jnp.float32)
    scale = 1.0 / math.sqrt(length)
    cosine = jnp.cos(phase) * scale
    sine = -jnp.sin(phase) * scale
    real = jnp.einsum("ft,ktrc->kfrc", cosine, block, precision=lax.Precision.HIGHEST)
    imag = jnp.einsum("ft,ktrc->kfrc", sine, block, precision=lax.Precision.HIGHEST)
    return jnp.stack([real, imag], axis=1)


def general_body(propagators, current_op):
    sym = 0.5 * (current_op + jnp.swapaxes(current_op, 1, 2))
    whole = lax.all_to_all(propagators, "col", split_axis=1, concat_axis=3, tiled=True)
    kdev = whole.shape[0]
    order = whole.shape[2]
    units = jnp.moveaxis(whole, 1, 0)
    total = units[0]
    identity = jnp.broadcast_to(jnp.eye(order, dtype=jnp.float32), total.shape)
    carry_in = prefix_2(total, ("tm", "col"), later_first, identity)
    _, applied = lax.scan(chain_step, carry_in, units)
    prefix = jnp.moveaxis(applied, 0, 1)
    weighted = jnp.einsum("kab,ksbc->ksac", sym, prefix, precision=lax.Precision.HIGHEST)
    n_rows = lax.axis_size("tm")
    n_cols = lax.axis_size("col")
    row_width = order // n_rows
    col_width = order // n_cols
    slices = prefix.shape[1]
    left = prefix.reshape(kdev, slices, order, n_rows, row_width)
    right = weighted.reshape(kdev, slices, order, n_cols, col_width)
    heis = jnp.einsum("ksbir,ksbjq->ksijrq", left, right, precision=lax.Precision.HIGHEST)
    heis = heis.reshape(kdev, slices, n_rows * n_cols, row_width, col_width)
    block = lax.all_to_all(heis, ("tm", "col"), split_axis=2, concat_axis=1, tiled=True)
    return spectrum_block(block[:, :, 0])


def halves(x):
    high = x.astype(jnp.bfloat16)
    return high, (x - high.astype(jnp.float32)).astype(jnp.bfloat16)


def as_left(x):
    high, low = halves(x)
    return jnp.concatenate([high, high, low], axis=1)


def as_right(x):
    high, low = halves(x)
    return jnp.concatenate([high, low, high], axis=0)


def as_right_t(x):
    high, low = halves(x)
    return jnp.concatenate([high, low, high], axis=1)


def product(left, right):
    return jnp.dot(left, right, preferred_element_type=jnp.float32)


def product_t(left, right):
    dims = (((1,), (1,)), ((), ()))
    return lax.dot_general(left, right, dims, preferred_element_type=jnp.float32)


VMEM = pl.BlockSpec(memory_space=pltpu.VMEM)


def local_call(kernel, outs, args, scratch=(), outside=()):
    near = [
        x if i in outside else pltpu.with_memory_space_constraint(x, pltpu.VMEM)
        for i, x in enumerate(args)
    ]
    return pl.pallas_call(
        kernel,
        out_shape=[pltpu.VMEM(s, jnp.float32) for s in outs],
        in_specs=[VMEM] * len(args),
        out_specs=[VMEM] * len(outs),
        scratch_shapes=list(scratch),
        compiler_params=GRANT,
    )(*near)


def pick_kernel(own, in_ref, out_ref, sems):
    core = lax.axis_index("col")
    source = in_ref.at[core if own else 1 - core]
    slices, part, _ = out_ref.shape
    copies = []
    for s in range(slices):
        for h in range(2):
            span = pl.ds(h * (part // 2), part // 2)
            copies.append(
                pltpu.make_async_copy(source.at[s, span, :], out_ref.at[s, span, :], sems.at[2 * s + h])
            )
            copies[-1].start()
    for copy in copies:
        copy.wait()


def start_kernel(mine_ref, got_ref, a0_ref, whole_ref, *refs):
    *prod_refs, a1_ref = refs
    core = lax.axis_index("col")
    part = got_ref.shape[1]
    for s, a_ref in enumerate((a0_ref, a1_ref)):
        a_ref[pl.ds(pl.multiple_of(core * part, 8), part), :] = mine_ref[s]
        a_ref[pl.ds(pl.multiple_of((1 - core) * part, 8), part), :] = got_ref[s]
    right = as_right(a1_ref[...])
    row = 0
    for p_ref in prod_refs:
        rows = p_ref.shape[0]
        part = product(as_left(a0_ref[row:row + rows, :]), right)
        p_ref[...] = part
        whole_ref[row:row + rows, :] = part
        row += rows


def packed(x):
    third = x.shape[0] // 3
    lower = jnp.concatenate([x[third:2 * third, third:], x[2 * third:, 2 * third:]], axis=1)
    return jnp.concatenate([x[:third, :], lower], axis=0)


def unpacked(x):
    third = x.shape[0] // 2
    top = x[:third, :]
    b11, b12, b22 = (x[third:, i * third:(i + 1) * third] for i in range(3))
    middle = jnp.concatenate([top[:, third:2 * third].T, b11, b12], axis=1)
    bottom = jnp.concatenate([top[:, 2 * third:].T, b12.T, b22], axis=1)
    return jnp.concatenate([top, middle, bottom], axis=0)


def local_kernel(*refs):
    a0_ref, b_ref, op_ref, sym_ref, g0_ref, g1_ref, pack_ref, own_ref, *row_refs = refs
    place = lax.axis_index("tm")
    op = op_ref[lax.axis_index("col")]
    sym = 0.5 * (op + op.T)
    sym_ref[...] = sym
    right = as_right(sym)
    for x_ref, g_ref in ((a0_ref, g0_ref), (b_ref, g1_ref)):
        x = x_ref[...]
        g_ref[...] = product_t(as_left(product(as_left(x), right)), as_right_t(x))
    rows = own_ref.shape[1]

    @pl.when(place >= 2)
    def _():
        pack_ref[0] = packed(g0_ref[...])
        pack_ref[1] = packed(g1_ref[...])

    @pl.when(place == 0)
    def _():
        own_ref[0] = g0_ref[:rows, :]
        own_ref[1] = g1_ref[:rows, :]
        for i, row_ref in enumerate(row_refs):
            row_ref[0] = g0_ref[(i + 1) * rows:(i + 2) * rows, :]


def hop_kernel(place, in_ref, step_ref, out_ref):
    @pl.when(lax.axis_index("tm") == place)
    def _():
        out_ref[...] = product(as_left(in_ref[...]), as_right(step_ref[...]))


def joined(out_ref, parts):
    row = 0
    for part in parts:
        out_ref[row:row + part.shape[0], :] = part[...]
        row += part.shape[0]


def rows_out(outs, wanted, heis, top, rows):
    for to, position in wanted.items():
        outs[to][position] = heis[to * rows - top:(to + 1) * rows - top, :]


def heis_kernel(place, receivers, count, chunks, *refs):
    sym_ref, g0_ref, g1_ref = refs[:3]
    before = refs[3:3 + chunks]
    outs, r_ref, t_ref = refs[3 + chunks:-2], refs[-2], refs[-1]
    outs = dict(zip(receivers, outs))

    @pl.when(lax.axis_index("tm") == place)
    def _():
        order = sym_ref.shape[0]
        rows = order // count
        joined(r_ref, before)
        t_ref[...] = as_right_t(r_ref[...])
        for i, middle_ref in enumerate((sym_ref, g0_ref, g1_ref)):
            t = 2 * place - 1 + i
            known = {to: heis_slices(place, to, count) for to in outs}
            wanted = {to: ts.index(t) for to, ts in known.items() if t in ts}
            if not wanted:
                continue
            top, bottom = min(wanted) * rows, (max(wanted) + 1) * rows
            weighted = product(as_left(r_ref[top:bottom, :]), as_right(middle_ref[...]))
            rows_out(outs, wanted, product_t(as_left(weighted), t_ref[...]), top, rows)


def last_kernel(count, chunks, *refs):
    sym_ref, g0_ref, g1_ref, step_ref = refs[:4]
    before = refs[4:4 + chunks]
    out_ref, r_ref, t_ref = refs[4 + chunks:]

    @pl.when(lax.axis_index("tm") == count - 1)
    def _():
        rows = out_ref.shape[1]
        top = (count - 1) * rows

        def own_rows(position, middle_ref):
            weighted = product(as_left(r_ref[top:, :]), as_right(middle_ref[...]))
            out_ref[position] = product_t(as_left(weighted), t_ref[...])

        joined(r_ref, before)
        t_ref[...] = as_right_t(r_ref[...])
        own_rows(0, sym_ref)
        r_ref[...] = product(as_left(r_ref[...]), as_right(step_ref[...]))
        t_ref[...] = as_right_t(r_ref[...])
        for i, middle_ref in enumerate((sym_ref, g0_ref, g1_ref)):
            own_rows(1 + i, middle_ref)


def ahead_kernel(place, count, chunks, *refs):
    pack_ref, *after = refs[:1 + chunks]
    outs, r_ref, t_ref = refs[1 + chunks:-2], refs[-2], refs[-1]

    @pl.when(lax.axis_index("tm") == place)
    def _():
        order = pack_ref.shape[2]
        rows = order // count
        joined(r_ref, after)
        t_ref[...] = as_right_t(r_ref[...])
        left = as_left(r_ref[:(place + 1) * rows, :])
        for i in range(2):
            weighted = product(left, as_right(unpacked(pack_ref[i])))
            heis = product_t(as_left(weighted), t_ref[...])
            rows_out(outs, {to: i for to in range(place + 1)}, heis, 0, rows)


def heis_slices(place, to, count):
    if to > place:
        return [2 * place] if place == count - 2 else [2 * place - 1, 2 * place]
    if to == place:
        return [2 * place - 3] * (place == count - 1) + [2 * place - 1, 2 * place, 2 * place + 1]
    return [2 * place, 2 * place + 1]


def heis_groups(place, count):
    if place == 1:
        return [[0], list(range(2, count)), [1]]
    return [list(range(place + 1, count)), [place]] if place + 1 < count else []


def gather_kernel(chosen, *refs):
    ins, (keep_ref, send_ref) = refs[:-2], refs[-2:]
    core = lax.axis_index("col")
    width = keep_ref.shape[2]
    for to, entries in enumerate(chosen):
        @pl.when(lax.axis_index("tm") == to)
        def _(entries=entries):
            for c in range(2):
                @pl.when(core == c)
                def _(c=c):
                    for slot, (_, source, i) in enumerate(entries):
                        block = ins[source][i]
                        keep_ref[slot] = block[:, c * width:(c + 1) * width]
                        send_ref[slot] = block[:, (1 - c) * width:(2 - c) * width]


def spectrum_kernel(own, tables, *refs):
    parts, (out_ref, all_ref, done_ref, sems) = refs[:2], refs[-4:]
    place, core = lax.axis_index("tm"), lax.axis_index("col")
    length, rows, _ = all_ref.shape
    for part, table in zip(parts, tables):
        for slot in range(part.shape[0]):
            t = sum(jnp.where(place == to, ts[slot], 0) for to, ts in enumerate(table))
            all_ref[t] = part[slot]
    scale = 1.0 / math.sqrt(length)
    step = 8
    groups = 3 if rows % (3 * step) == 0 else 1
    size = rows // groups

    def cosine(n):
        return scale * math.cos(2.0 * math.pi * (n % length) / length)

    def sine(n):
        return scale * math.sin(2.0 * math.pi * (n % length) / length)

    def turn(row, carry):
        here = pl.ds(pl.multiple_of(row * step, step), step)
        values = [all_ref[t, here, :] for t in range(length)]
        for f in range(length // 2 + 1):
            real = sum(cosine(f * t) * values[t] for t in range(length))
            imag = sum(-sine(f * t) * values[t] for t in range(length))
            done_ref[0, f, here, :] = real
            done_ref[1, f, here, :] = imag
            mirrored = (length - f) % length
            if mirrored != f:
                done_ref[0, mirrored, here, :] = real
                done_ref[1, mirrored, here, :] = -imag
        return carry

    copies = []
    for g in range(groups):
        lax.fori_loop(g * size // step, (g + 1) * size // step, turn, 0)
        span = pl.ds(g * size, size)
        copy = pltpu.make_async_copy(
            done_ref.at[:, :, span, :], out_ref.at[core if own else 1 - core, :, :, span, :], sems.at[g]
        )
        copy.start()
        copies.append(copy)
    for copy in copies:
        copy.wait()


def paired_body(propagators, current_op):
    count = lax.axis_size("tm")
    flipped = jnp.swapaxes(propagators, 2, 3)
    kdev, slices, part, order = flipped.shape
    rows = order // count
    step = order // CHUNKS
    square, chunk = (order, order), (step, order)
    swap = [(0, 1), (1, 0)]
    scratch = [pltpu.VMEM(square, jnp.float32), pltpu.VMEM((order, 3 * order), jnp.bfloat16)]

    def pick(own):
        return pl.pallas_call(
            lambda *r: pick_kernel(own, *r),
            out_shape=pltpu.VMEM((slices, part, order), jnp.float32),
            in_specs=[pl.BlockSpec(memory_space=pltpu.HBM)],
            out_specs=VMEM,
            scratch_shapes=[pltpu.SemaphoreType.DMA((2 * slices,))],
            compiler_params=GRANT,
        )(pltpu.with_memory_space_constraint(flipped, pltpu.HBM))

    got = lax.ppermute(pick(False), "col", swap)
    mine = pick(True)
    a0, whole, *prod = local_call(
        start_kernel, [square] * 2 + [chunk] * CHUNKS, (mine, got),
        scratch=[pltpu.VMEM(square, jnp.float32)],
    )

    def along(x, hop):
        return lax.ppermute(x, "tm", [hop] if isinstance(hop, tuple) else hop)

    arrays, plan = [], [[] for _ in range(count)]

    def keep(x, to, ts, rank):
        plan[to].extend((rank, t, len(arrays), i) for i, t in enumerate(ts))
        arrays.append(x)

    soon = [(1, 0)]
    before = [along(x, (0, 1)) for x in prod]
    shapes = [square] * 3 + [(2, 2 * (order // 3), order), (2, rows, order)] + [(1, rows, order)] * (count - 1)
    sym, g0, g1, pack, own, *firsts = local_call(local_kernel, shapes, (a0, whole, current_op), outside=(2,))
    last_step = along(whole, (count - 2, count - 1))
    ahead = along(pack, [(j, j - 1) for j in range(2, count)])
    keep(own, 0, [0, 1], 0)
    for to in range(1, count):
        keep(along(firsts[to - 1], (0, to)), to, [0], 1 if to == 1 else 5)
    for place in range(1, count - 1):
        after = []
        for x in before:
            after += local_call(lambda *r, p=place: hop_kernel(p, *r), [chunk], (x, whole))
        passed = after if place < count - 2 else before
        following = [along(x, (place, place + 1)) for x in passed]
        for receivers in heis_groups(place, count):
            outs = local_call(
                lambda *r, p=place, w=receivers: heis_kernel(p, w, count, CHUNKS, *r),
                [(len(heis_slices(place, to, count)), rows, order) for to in receivers],
                (sym, g0, g1, *before), scratch=scratch,
            )
            for to, x in zip(receivers, outs):
                ts = heis_slices(place, to, count)
                if to == place:
                    keep(x, to, ts, 0)
                else:
                    keep(along(x, (place, to)), to, ts, 1 if (place, to) in soon else 3)
        outs = local_call(
            lambda *r, p=place: ahead_kernel(p, count, CHUNKS, *r),
            [(2, rows, order)] * (place + 1), (ahead, *after), scratch=scratch,
        )
        for to, x in enumerate(outs):
            ts = [2 * place + 2, 2 * place + 3]
            if to == place:
                keep(x, to, ts, 2)
            else:
                keep(along(x, (place, to)), to, ts, 4)
        before = following
    last_slices = heis_slices(count - 1, count - 1, count)
    outs = local_call(
        lambda *r: last_kernel(count, CHUNKS, *r), [(len(last_slices), rows, order)],
        (sym, g0, g1, last_step, *before), scratch=scratch,
    )
    keep(outs[0], count - 1, last_slices, 0)
    width = order // 2
    length = count * slices
    half = length // 2
    ordered = [[entry[1:] for entry in sorted(entries)] for entries in plan]
    kept, taken, tables = [], [], []
    for chosen in ([o[:half] for o in ordered], [o[half:] for o in ordered]):
        used = sorted({source for entries in chosen for _, source, _ in entries})
        local = [[(t, used.index(source), i) for t, source, i in entries] for entries in chosen]
        mine_part, give = local_call(
            lambda *r, c=local: gather_kernel(c, *r), [(half, rows, width)] * 2,
            [arrays[source] for source in used],
        )
        taken.append(lax.ppermute(give, "col", swap))
        kept.append(mine_part)
        tables.append([[t for t, _, _ in entries] for entries in chosen])

    def spectrum(own, parts, so_far):
        return pl.pallas_call(
            lambda *r: spectrum_kernel(own, tables, *r),
            out_shape=jax.ShapeDtypeStruct((kdev, 2, length, rows, width), jnp.float32),
            in_specs=[VMEM] * 2 + [pl.BlockSpec(memory_space=pl.ANY)] * len(so_far),
            out_specs=pl.BlockSpec(memory_space=pl.ANY),
            scratch_shapes=[
                pltpu.VMEM((length, rows, width), jnp.float32),
                pltpu.VMEM((2, length, rows, width), jnp.float32),
                pltpu.SemaphoreType.DMA((3,)),
            ],
            input_output_aliases={2: 0} if so_far else {},
            compiler_params=GRANT,
            name="spectrum",
        )(*(pltpu.with_memory_space_constraint(x, pltpu.VMEM) for x in parts), *so_far)

    return spectrum(False, taken, [spectrum(True, kept, [])])


def is_paired(mesh, kdev, slices, order):
    count = mesh.shape["tm"]
    fits = kdev == 2 and mesh.shape["col"] == 2 and slices == 2 and count > 2
    return fits and order % 384 == 0 and order % (16 * CHUNKS) == 0 and order % (16 * count) == 0


def solution(mesh):
    def body(propagators, current_op):
        kdev, slices, order, _ = propagators.shape
        if is_paired(mesh, kdev, slices, order):
            return paired_body(propagators, current_op)
        return general_body(propagators, current_op)

    return jax.shard_map(
        body,
        mesh=mesh,
        in_specs=(P(("drive", "mom"), "tm", None, "col"), P("mom", None, None)),
        out_specs=P(("drive", "mom"), None, None, "tm", "col"),
        check_vma=False,
    )
```
